32 devices in a mesh: dp: 4 (over x, core), fsdp: 8 (over z, y).
Axes of the slice: x: 2, y: 2, z: 4, core: 2. Of those that a mesh axis runs over, the one named last changes fastest.
Arguments:
- queries: bfloat16 [64, 128, 1280], P(('dp', 'fsdp')), may hold values from -100 to 100
- keys: bfloat16 [64, 128, 1280], P(('dp', 'fsdp')), may hold values from -100 to 100
- values: bfloat16 [64, 128, 1280], P(('dp', 'fsdp')), may hold values from -64 to 64
- block_len: int32 [64], P(('dp', 'fsdp')), may hold values from 0 to 128, as said below
- target: int32 [64], P(('dp', 'fsdp')), may hold values from 0 to 2, as said below
- cotangent: bfloat16 [32, 128, 1280], P(('dp', 'fsdp')), may hold values from -6 to 6
- out_weight: bfloat16 [1280, 1280], P('fsdp'), may hold values from -0.15625 to 0.15625
Outputs:
- embedding: bfloat16 [32, 128, 1280], P(('dp', 'fsdp'))
- weight_grad: float32 [1280, 1280], P('fsdp')
The draws below stay inside these ranges and needn't reach their ends.
Inputs may be any that keep to these rules, and one draw needn't show every extreme that they name: `block_len`: 0 exactly in the empty slots, those with target 2; live blocks hold 1 to 128 patches; in every draw some device has all its slots live and full. `target`: t < 1: output slot t of the same device; 1 <= t < 2: output slot t - 1 of the next device along dp (wrapping), same fsdp index; t = 2: empty slot; live values are distinct within a device, every output slot receives exactly one block, and in every draw some device has all 2 slots live.
All inputs are finite; a program needn't handle non-finite values.
Results may differ from the reference program's by a relative error of at most 0.012.
Values may be sent and summed in bfloat16 or wider, within the bound.
A program may use at most 64 MiB of HBM per device.

```python
import jax
import jax.numpy as jnp
from jax import lax

D = 1280
HEADS = 16
HEAD_DIM = 80
WIN = 128
OUT_DEV = 1
SLOTS = 2
IN_BLOCKS = 64
OUT_BLOCKS = 32
N_DP = 4
N_FSDP = 8
DEVICES = 32


def attention_pair(key):
    base = jax.random.fold_in(key, 101)
    key_query, key_key = jax.random.split(base, 2)
    shape = (IN_BLOCKS, WIN, HEADS, HEAD_DIM)
    query_draw = jnp.clip(jax.random.normal(key_query, shape, jnp.float32), -6.0, 6.0)
    key_draw = jnp.clip(jax.random.normal(key_key, shape, jnp.float32), -6.0, 6.0)
    return (query_draw.reshape(IN_BLOCKS, WIN, D), key_draw.reshape(IN_BLOCKS, WIN, D))


def draw_queries(key, part):
    return attention_pair(key)[0].astype(jnp.bfloat16)


def draw_keys(key, part):
    return attention_pair(key)[1].astype(jnp.bfloat16)


def draw_values(key, part):
    base = jax.random.fold_in(key, 303)
    key_noise, key_head = jax.random.split(base, 2)
    head_index = jnp.arange(HEADS, dtype=jnp.float32) / max(HEADS - 1, 1)
    jitter = jnp.exp(0.25 * jnp.clip(jax.random.normal(key_head, (HEADS,), jnp.float32), -2.0, 2.0))
    shape = (IN_BLOCKS, WIN, HEADS, HEAD_DIM)
    head_scale = 0.5 * jnp.power(3.0, head_index) * jitter
    noise = jnp.clip(jax.random.normal(key_noise, shape, jnp.float32), -6.0, 6.0)
    drawn = noise * head_scale[:, None]
    return drawn.reshape(IN_BLOCKS, WIN, D).astype(jnp.bfloat16)


def routing(key):
    base = jax.random.fold_in(key, 202)
    key_left, key_forced, key_order, key_full, key_short = jax.random.split(base, 5)
    from_left = jax.random.randint(key_left, (N_DP, N_FSDP, OUT_DEV), 0, 2)
    forced = jax.random.randint(key_forced, (), 0, N_DP)
    cycle_index = jnp.arange(N_DP, dtype=jnp.int32)[:, None, None]
    from_left = jnp.where(cycle_index == forced, 0, from_left)
    from_left = jnp.where(cycle_index == (forced + 1) % N_DP, 1, from_left)
    next_left = jnp.roll(from_left, -1, axis=0)
    occupied = jnp.concatenate([from_left == 0, next_left == 1], axis=2)
    scores = jax.random.randint(key_order, (N_DP, N_FSDP, SLOTS), 0, 1 << 20) * SLOTS + jnp.arange(SLOTS, dtype=jnp.int32)
    ordering = jnp.argsort(scores, axis=2).astype(jnp.int32)
    occupied_slot = jnp.take_along_axis(occupied, ordering, axis=2)
    full_pick = jax.random.randint(key_full, (N_DP, N_FSDP, SLOTS), 0, 4)
    short_len = jax.random.randint(key_short, (N_DP, N_FSDP, SLOTS), 1, WIN + 1)
    lengths = jnp.where(full_pick < 3, WIN, short_len)
    lengths = jnp.where(cycle_index == forced, WIN, lengths)
    target_out = jnp.where(occupied_slot, ordering, SLOTS).astype(jnp.int32).reshape(IN_BLOCKS)
    length_out = jnp.where(occupied_slot, lengths, 0).astype(jnp.int32).reshape(IN_BLOCKS)
    return (target_out, length_out)


def draw_block_len(key, part):
    return routing(key)[1]


def draw_target(key, part):
    return routing(key)[0]


def block_scale(key, shape, cuts, least, high):
    factor_of, own = 1.0, jax.random.fold_in(key, 6)
    for dim, parts in cuts:
        heights = jnp.exp(jax.random.uniform(jax.random.fold_in(own, dim), (parts,), jnp.float32, least / len(cuts), high / len(cuts)))
        factor_of = factor_of * jnp.repeat(heights, shape[dim] // parts).reshape([-1 if axis == dim else 1 for axis in range(len(shape))])
    return factor_of


def normal_values(own_key, extent, spread, limit, pieces=(), kind=jnp.bfloat16):
    result = spread * jax.random.normal(own_key, extent, jnp.float32)
    if pieces:
        result = result * block_scale(own_key, extent, pieces, -0.22, 0.18)
    return jnp.clip(result, -limit, limit).astype(kind)


def setup_inputs(seed: int = 0) -> dict:
    arg_keys = jax.random.split(jax.random.key(seed), 8)
    queries = draw_queries(jax.random.fold_in(arg_keys[7], 71), 0)
    keys = draw_keys(jax.random.fold_in(arg_keys[7], 71), 0)
    values = draw_values(jax.random.fold_in(arg_keys[7], 71), 0)
    block_len = draw_block_len(jax.random.fold_in(arg_keys[7], 71), 0)
    target = draw_target(jax.random.fold_in(arg_keys[7], 71), 0)
    cotangent = normal_values(arg_keys[5], (OUT_BLOCKS, WIN, D), 1.0, 6.0, ((0, 32),))
    out_weight = normal_values(arg_keys[6], (D, D), D ** -0.5, 0.15625, ((0, 8),))
    return {"queries": queries, "keys": keys, "values": values, "block_len": block_len, "target": target, "cotangent": cotangent, "out_weight": out_weight}


def attend_block(query, key_block, value_block, length):
    shape = (WIN, HEADS, HEAD_DIM)
    query_heads = query.reshape(shape).astype(jnp.float32)
    key_heads = key_block.reshape(shape).astype(jnp.float32)
    value_heads = value_block.reshape(shape).astype(jnp.float32)
    scores = jnp.einsum('qhd,khd->hqk', query_heads, key_heads) * HEAD_DIM ** (-0.5)
    position = jnp.arange(WIN, dtype=jnp.int32)
    usable = position < length
    scores = jnp.where(usable[None, None, :], scores, -1e+30)
    highest = lax.optimization_barrier(jnp.max(scores, axis=-1, keepdims=True))
    exponent = jnp.exp(scores - highest)
    attn_weights = (exponent / lax.optimization_barrier(jnp.sum(exponent, axis=-1, keepdims=True))).astype(jnp.bfloat16)
    mixed_out = jnp.einsum('hqk,khd->qhd', attn_weights.astype(jnp.float32), value_heads)
    mixed_out = jnp.where(usable[:, None, None], mixed_out, 0.0)
    return mixed_out.reshape(WIN, D).astype(jnp.bfloat16)

def reference(queries, keys, values, block_len, target, cotangent, out_weight):
    attended_in = lax.map(lambda item: attend_block(item[0], item[1], item[2], item[3]), (queries, keys, values, block_len))
    block_index = jnp.arange(IN_BLOCKS, dtype=jnp.int32)
    device = block_index // SLOTS
    cycle_index = device // N_FSDP
    column = device % N_FSDP
    step_over = target // OUT_DEV
    out_slot = target % OUT_DEV
    owner = (cycle_index + step_over) % N_DP
    destination = (owner * N_FSDP + column) * OUT_DEV + out_slot
    destination = jnp.where(target == SLOTS, OUT_BLOCKS, destination).astype(jnp.int32)
    placed = jnp.zeros((OUT_BLOCKS, WIN, D), jnp.bfloat16).at[destination].set(attended_in, mode='drop')
    flat_rows = placed.reshape(OUT_BLOCKS * WIN, D)
    embedding = jnp.dot(flat_rows, out_weight, preferred_element_type=jnp.float32).astype(jnp.bfloat16)
    embedding = embedding.reshape(OUT_BLOCKS, WIN, D)
    per_device = flat_rows.reshape(DEVICES, OUT_DEV * WIN, D)
    cot_device = cotangent.reshape(DEVICES, OUT_DEV * WIN, D)

    def accumulate(running, item):
        partial_grad = jnp.dot(item[0].T, item[1], preferred_element_type=jnp.float32)
        rounded = lax.optimization_barrier(partial_grad.astype(jnp.bfloat16)).astype(jnp.float32)
        return (running + rounded, None)
    raw_grad, unused = lax.scan(accumulate, jnp.zeros((D, D), jnp.float32), (per_device, cot_device))
    grad_norm = jnp.sqrt(jnp.sum(raw_grad * raw_grad) + 1e-06)
    weight_grad = raw_grad * jnp.minimum(1.0, D / grad_norm)
    return (embedding, weight_grad)
```

```python
import functools
import math

import jax
import jax.numpy as jnp
from jax import lax
from jax.experimental import pallas as pl
from jax.experimental.pallas import tpu as pltpu
from jax.sharding import PartitionSpec as P

HEADS = 16
LANES = 128
MESH = pl.DeviceIdType.MESH
F32 = jnp.float32
BF16 = jnp.bfloat16


def starts_of(width, group):
    tiles = width // LANES
    window = -(-tiles // group) * LANES
    return window, [min(i * window, width - window) for i in range(group)]


def marks_of(width):
    tiles = width // LANES
    return [tiles * tenths // 10 * LANES for tenths in (0, 4, 7, 9, 10)]


def kernel(
    n_dp, n_fs, group, finish,
    len_ref, tgt_ref, q_ref, k_ref, v_ref, cot_ref, w_ref,
    emb_ref, grad_ref, factor_ref,
    wq, cq, mine, nxt, arr, placed, gpart, yrecv, zsend, zrecv, esend, ebuf, tbuf, sbuf, srecv, gsum,
    wz_s, wz_r, wy_s, wy_r, c_s, c_r, n_s, n_r, p_s, p_r, gy_s, gy_r, gz_s, gz_r,
    e_s, e_r, t_s, t_r, q_s, q_r, m_s, m_r,
):
    slots, rows, width = q_ref.shape
    shard = w_ref.shape[0]
    hd = width // HEADS
    window, starts = starts_of(width, group)
    over = group * window - width
    nz = n_fs // 2
    d, f = lax.axis_index("dp"), lax.axis_index("fsdp")
    base = (d // group) * group
    gi = d - base
    z, y = f // 2, f % 2
    other = z * 2 + (1 - y)
    ahead, behind = (d + 1) % n_dp, (d + n_dp - 1) % n_dp
    mates = [(gi + j) % group for j in range(1, group)]
    core, side = gi % 2, gi // 2
    partner, across = side * 2 + (1 - core), (1 - side) * 2 + core

    def start_of(i):
        if group == 1:
            return 0
        return pl.multiple_of(i * window - (i // (group - 1)) * over, LANES)

    def copy(src, dst, s, r, to):
        return pltpu.make_async_remote_copy(
            src_ref=src, dst_ref=dst, send_sem=s, recv_sem=r, device_id=to, device_id_type=MESH
        )

    def spread(at, s, r):
        to = [partner, across] if group == 4 else mates
        made = [copy(at(gi), at(gi), s(j), r(j), (base + m, f)) for j, m in enumerate(to)]
        for c in made:
            c.start()
        return made

    def relay(made, at, s, r):
        if group != 4:
            return made
        made[1].wait_recv()
        c = copy(at(across), at(across), s(2), r(2), (base + partner, f))
        c.start()
        made.append(c)
        return [made[0], c]

    barrier = pltpu.get_barrier_semaphore()
    peers = [(ahead, f), (behind, f)]
    peers += [(base + m, f) for m in mates]
    peers += [(d, (f + j) % n_fs) for j in range(1, n_fs)]
    for peer in peers:
        pl.semaphore_signal(barrier, inc=1, device_id=peer, device_id_type=MESH)

    my_cols = pl.ds(start_of(gi), window)
    my_rows = pl.ds(pl.multiple_of(gi * rows, rows), rows)

    def w_at(index):
        return wq.at[pl.ds(pl.multiple_of(index * shard, shard), shard), :]

    wz, wy, cots = [], [], []

    def open_links():
        pl.semaphore_wait(barrier, len(peers))
        w_src = w_ref.at[:, my_cols]
        for j in range(1, nz):
            c = copy(w_src, w_at(f), wz_s.at[j], wz_r.at[j], (d, ((z + j) % nz) * 2 + y))
            c.start()
            wz.append(c)
        wy.append(copy(w_src, w_at(f), wy_s.at[0], wy_r.at[0], (d, other)))
        wy[0].start()
        for j, m in enumerate(mates):
            c = copy(
                cot_ref.at[0, :, pl.ds(start_of(m), window)], cq.at[my_rows, :],
                c_s.at[j], c_r.at[j], (base + m, f),
            )
            c.start()
            cots.append(c)
        wq[pl.ds(pl.multiple_of(f * shard, shard), shard), :] = w_ref[:, my_cols]
        cq[my_rows, :] = cot_ref[0, :, my_cols]

    key_pos = lax.broadcasted_iota(jnp.int32, (rows, rows), 1)
    row_pos = lax.broadcasted_iota(jnp.int32, (rows, LANES), 0)
    lens = [len_ref[s] for s in range(slots)]
    usable = [key_pos < lens[s] for s in range(slots)]
    limit = [[jnp.where(tgt_ref[s] == t, lens[s], 0) for s in range(slots)] for t in range(2)]
    keep = [[row_pos < limit[t][s] for s in range(slots)] for t in range(2)]
    tiles = {}
    marks = marks_of(width)
    parts = len(marks) - 1
    nexts, cast_all = [], []

    def send_next(part):
        cols = pl.ds(marks[part], marks[part + 1] - marks[part])
        c = copy(nxt.at[:, cols], arr.at[:, cols], n_s.at[part], n_r.at[part], (ahead, f))
        c.start()
        nexts.append(c)

    def placed_at(part):
        cols = pl.ds(marks[part], marks[part + 1] - marks[part])
        return lambda i: placed.at[pl.ds(pl.multiple_of(i * rows, rows), rows), cols]

    def cast(part):
        nexts[part].wait_recv()
        cols = pl.ds(marks[part], marks[part + 1] - marks[part])
        placed[my_rows, cols] = mine[:, cols] + arr[:, cols]
        return spread(placed_at(part), lambda j: p_s.at[part, j], lambda j: p_r.at[part, j])

    def hand_on(part, made):
        return relay(
            made, placed_at(part), lambda j: p_s.at[part, j], lambda j: p_r.at[part, j]
        )

    for h in range(HEADS):
        first, last = h * hd, (h + 1) * hd
        lo, hi = first // LANES * LANES, -(-last // LANES) * LANES
        lane = lax.broadcasted_iota(jnp.int32, (rows, hi - lo), 1) + lo
        inside = (lane >= first) & (lane < last)
        for s in range(slots):
            query = jnp.where(inside, q_ref[s, :, lo:hi].astype(F32), 0.0).astype(BF16)
            scores = lax.dot_general(
                query, k_ref[s, :, lo:hi], (((1,), (1,)), ((), ())), preferred_element_type=F32
            ) * hd ** (-0.5)
            scores = jnp.where(usable[s], scores, -1e30)
            exponent = jnp.exp(scores - jnp.max(scores, axis=-1, keepdims=True))
            weights = (exponent / jnp.sum(exponent, axis=-1, keepdims=True)).astype(BF16)
            mixed = jnp.dot(weights, v_ref[s, :, lo:hi], preferred_element_type=F32)
            mixed = jnp.where(inside, mixed, 0.0)
            for t in range(lo // LANES, hi // LANES):
                piece = mixed[:, t * LANES - lo:(t + 1) * LANES - lo]
                tiles[s, t] = tiles[s, t] + piece if (s, t) in tiles else piece
        for t in range(lo // LANES, hi // LANES):
            if (t + 1) * LANES <= last:
                cols = slice(t * LANES, (t + 1) * LANES)
                for dest, ref in ((0, mine), (1, nxt)):
                    total = sum(
                        jnp.where(keep[dest][s], tiles[s, t], 0.0) for s in range(slots)
                    )
                    ref[:, cols] = total.astype(BF16)
        if h == HEADS // 8 - 1:
            open_links()
        ready = last // LANES * LANES
        while len(nexts) < parts - 1 and marks[len(nexts) + 1] <= ready:
            send_next(len(nexts))
            if len(nexts) > 1:
                cast_all.append(cast(len(nexts) - 2))
    send_next(parts - 1)
    cast_all.append(cast(parts - 2))
    waits = hand_on(0, cast_all[0])
    cast_all.append(cast(parts - 1))
    for j in range(1, nz):
        wz[j - 1].wait_recv()
        from_f = ((z + nz - j) % nz) * 2 + y
        c = copy(w_at(from_f), w_at(from_f), wy_s.at[j], wy_r.at[j], (d, other))
        c.start()
        wy.append(c)

    for part in range(1, parts):
        waits += hand_on(part, cast_all[part])
    casts = sum(cast_all, [])
    for c in cots + waits:
        c.wait_recv()

    step = 2 * LANES
    for i in range(width // step):
        gpart[i * step:(i + 1) * step, :] = lax.dot_general(
            placed[:, i * step:(i + 1) * step], cq[...], (((0,), (0,)), ((), ())),
            preferred_element_type=F32,
        ).astype(BF16)

    def g_rows(index):
        return pl.ds(pl.multiple_of(index * shard, shard), shard)

    order = list(range(1, nz)) + [0]
    gy = []
    for j in order:
        zj = (z + j) % nz
        c = copy(
            gpart.at[g_rows(zj * 2 + (1 - y)), :], yrecv.at[zj],
            gy_s.at[j], gy_r.at[j], (d, other),
        )
        c.start()
        gy.append(c)
    gz = []
    for j, c in zip(order, gy):
        zj = (z + j) % nz
        c.wait_recv()
        pair = gpart[g_rows(zj * 2 + y), :].astype(F32) + yrecv[zj].astype(F32)
        if j == 0:
            own = pair
        else:
            zsend[j] = pair.astype(BF16)
            c = copy(zsend.at[j], zrecv.at[j], gz_s.at[j], gz_r.at[j], (d, zj * 2 + y))
            c.start()
            gz.append(c)

    for c in wy:
        c.wait_recv()
    embs = []
    for i in range(group):
        esend[i] = jnp.dot(
            placed[i * rows:(i + 1) * rows, :], wq[...], preferred_element_type=F32
        ).astype(BF16)
    for j, m in enumerate(mates):
        c = copy(esend.at[m], ebuf.at[gi], e_s.at[j], e_r.at[j], (base + m, f))
        c.start()
        embs.append(c)
    ebuf[gi] = esend[gi]

    for c in gz:
        c.wait_recv()
    for j in range(1, nz):
        own = own + zrecv[j].astype(F32)
    ends = starts[1:] + [width]
    tbuf[gi] = own.astype(BF16)
    turn_at = lambda i: tbuf.at[i]
    turn_s, turn_r = (lambda j: t_s.at[j]), (lambda j: t_r.at[j])
    turns = spread(turn_at, turn_s, turn_r)
    squares = []
    if finish:
        valid = window
        for i in range(group):
            valid = jnp.where(gi == i, ends[i] - starts[i], valid)
        lane = lax.broadcasted_iota(jnp.int32, (8, LANES), 1)
        total = jnp.zeros((8, LANES), F32)
        for col in range(0, window, LANES):
            tile = own[:, col:col + LANES].astype(BF16).astype(F32)
            part = jnp.sum((tile * tile).reshape(shard // 8, 8, LANES), axis=0)
            total = total + jnp.where(lane + col < valid, part, 0.0)
        sbuf[...] = total
        for j in range(1, n_fs):
            c = copy(sbuf, srecv.at[j], q_s.at[j], q_r.at[j], (d, (f + j) % n_fs))
            c.start()
            squares.append(c)
    waits = relay(turns, turn_at, turn_s, turn_r)
    if finish:
        for j, c in zip(range(1, n_fs), squares):
            c.wait_recv()
            total = total + srecv[j]
        gsum[gi] = total
        for j, m in enumerate(mates):
            c = copy(gsum.at[gi], gsum.at[gi], m_s.at[j], m_r.at[j], (base + m, f))
            c.start()
            squares.append(c)
    for c in embs:
        c.wait_recv()
    for i in range(group):
        emb_ref[0, :, starts[i]:ends[i]] = ebuf[i, :, 0:ends[i] - starts[i]]
    for c in waits:
        c.wait_recv()
    if finish:
        for c in squares[n_fs - 1:]:
            c.wait_recv()
        total = gsum[0]
        for i in range(1, group):
            total = total + gsum[i]
        norm = jnp.sqrt(jnp.sum(total, keepdims=True) + 1e-06)
        factor = jnp.minimum(1.0, float(width) / norm)
    for i in range(group):
        grad_ref[:, starts[i]:ends[i]] = tbuf[i, :, 0:ends[i] - starts[i]]
    factor_ref[...] = jnp.broadcast_to(factor, factor_ref.shape) if finish else jnp.ones_like(factor_ref)
    for c in wz + wy + cots + nexts + casts + gy + gz + embs + turns + squares:
        c.wait_send()


CUTS = (0, 2, 4, 6, 8)
OPEN = 1
PLAN = [
    ((0, 3), "send", 0), ((0, 7), "send", 1), ((1, 3), "pass", 0), ((1, 3), "send", 2),
    ((1, 5), "w", 1), ((1, 6), "pass", 1), ((1, 6), "w", 2), ((1, 7), "send", 3),
]


def kernel_quad(
    n_fs,
    len_ref, tgt_ref, q_ref, k_ref, v_ref, cot_ref, w_ref,
    emb_ref, grad_ref, factor_ref,
    att, got, placed, cots, wq, gpart, yrecv, zsend, zrecv, esend, ebuf, eown, turned, srecv,
    wz_s, wz_r, wy_s, wy_r, c_s, c_r, kc_s, kc_r, kx_s, kx_r, kf_s, kf_r,
    gy_s, gy_r, gz_s, gz_r, e_s, e_r, t_s, t_r, q_s, q_r,
):
    slots, rows, width = q_ref.shape
    hd = width // HEADS
    half = width // 2
    nz = n_fs // 2
    nh = nz // 2
    per = n_fs // 2
    d, f = lax.axis_index("dp"), lax.axis_index("fsdp")
    x, c = d // 2, d % 2
    z, y = f // 2, f % 2
    partner, across = 2 * x + 1 - c, 2 * (1 - x) + c
    other = 2 * z + 1 - y
    halves = [1 - z // nh, z // nh]

    def copy(src, dst, s, r, to):
        return pltpu.make_async_remote_copy(
            src_ref=src, dst_ref=dst, send_sem=s, recv_sem=r, device_id=to, device_id_type=MESH
        )

    sent = []

    def start(*args):
        made = copy(*args)
        made.start()
        sent.append(made)
        return made

    barrier = pltpu.get_barrier_semaphore()
    peers = [((d + i) % 4, (f + j) % n_fs) for i in range(4) for j in range(n_fs) if i or j]
    for peer in peers:
        pl.semaphore_signal(barrier, inc=1, device_id=peer, device_id_type=MESH)

    def side(i):
        return pl.ds(pl.multiple_of(i * half, LANES), half)

    def shard_half(i):
        return pl.ds(pl.multiple_of(i * hd, 16), hd)

    def block(i):
        return pl.ds(pl.multiple_of(i * rows, rows), rows)

    wz, wy, cot_in = [], [], []

    def open_links():
        pl.semaphore_wait(barrier, len(peers))
        for j in (2, 1, 3):
            m = (d + j) % 4
            cot_in.append(start(
                cot_ref.at[0, :, side(m % 2)], cots.at[block(d), :], c_s.at[j], c_r.at[j], (m, f)
            ))
        w_src = w_ref.at[shard_half(x), side(c)]
        for j in range(1, nz):
            wz.append(start(
                w_src, wq.at[f], wz_s.at[j], wz_r.at[j], (d, ((z + j) % nz) * 2 + y)
            ))
        wy.append(start(w_src, wq.at[f], wy_s.at[0], wy_r.at[0], (d, other)))
        wq[f] = w_ref[shard_half(x), side(c)]
        cots[block(d), :] = cot_ref[0, :, side(c)]

    def pass_weight(j):
        wz[j - 1].wait_recv()
        from_f = ((z + nz - j) % nz) * 2 + y
        wy.append(start(wq.at[from_f], wq.at[from_f], wy_s.at[j], wy_r.at[j], (d, other)))

    key_pos = lax.broadcasted_iota(jnp.int32, (rows, rows), 0)
    row_pos = lax.broadcasted_iota(jnp.int32, (hd, rows), 1)
    lens = [len_ref[s] for s in range(slots)]
    usable = [key_pos < lens[s] for s in range(slots)]
    keep = [
        [row_pos < jnp.where(tgt_ref[s] == t, lens[s], 0) for s in range(slots)] for t in range(2)
    ]
    scale = hd ** (-0.5) * math.log2(math.e)
    turned_v = {}

    def value_rows(step, s, first, last):
        found = []
        for t in range(first // LANES, -(-last // LANES)):
            if (step, s, t) not in turned_v:
                at = pl.ds(pl.multiple_of(halves[step] * half + t * LANES, LANES), LANES)
                turned_v[step, s, t] = v_ref[s, :, at].T
            a, b = max(first - t * LANES, 0), min(last - t * LANES, LANES)
            found.append(turned_v[step, s, t][a:b, :])
        return found[0] if len(found) == 1 else jnp.concatenate(found, axis=0)

    def attend(step, h):
        first, last = h * hd, (h + 1) * hd
        lo, hi = first // LANES * LANES, -(-last // LANES) * LANES
        at = pl.ds(pl.multiple_of(halves[step] * half + lo, LANES), hi - lo)
        lane = lax.broadcasted_iota(jnp.int32, (rows, hi - lo), 1) + lo
        inside = ((lane >= first) & (lane < last)).astype(F32).astype(BF16)
        mixed = []
        for s in range(slots):
            scores = lax.dot_general(
                k_ref[s, :, at], q_ref[s, :, at] * inside, (((1,), (1,)), ((), ())),
                preferred_element_type=F32,
            )
            scores = jnp.where(usable[s], scores, -1e30)
            exponent = jnp.exp2((scores - jnp.max(scores, axis=0, keepdims=True)) * scale)
            inverse = 1.0 / jnp.sum(exponent, axis=0, keepdims=True)
            weights = (exponent * inverse).astype(BF16)
            mixed.append(jnp.dot(
                value_rows(step, s, first, last), weights, preferred_element_type=F32
            ))
        for t in range(2):
            total = sum(jnp.where(keep[t][s], mixed[s], 0.0) for s in range(slots))
            att[t, h % 2, step * per + h // 2] = total.astype(BF16)

    cuts = CUTS
    core_in, x_in, f_in = [], [], []

    def send_chunk(k):
        a, n = cuts[k], cuts[k + 1] - cuts[k]
        at = pl.ds(a, n)
        core_in.append(start(
            att.at[:, x, at], got.at[d, :, at], kc_s.at[k], kc_r.at[k], (partner, f)
        ))
        x_in.append(start(
            att.at[:, 1 - x, at], got.at[d, :, at], kx_s.at[k], kx_r.at[k], (across, f)
        ))
        for t in range(2):
            got[d, t, at] = att[t, x, at]

    def pass_chunk(k):
        at = pl.ds(cuts[k], cuts[k + 1] - cuts[k])
        x_in[k].wait_recv()
        f_in.append(start(
            got.at[across, :, at], got.at[across, :, at], kf_s.at[k], kf_r.at[k], (partner, f)
        ))

    def combine(k):
        core_in[k].wait_recv()
        f_in[k].wait_recv()
        for s in range(cuts[k], cuts[k + 1]):
            index = halves[s // per] * per + s % per
            for b in range(4):
                placed[index, :, b * rows:(b + 1) * rows] = got[b, 0, s] + got[(b + 3) % 4, 1, s]

    gy = {}

    def gradient(step):
        mat = placed[pl.ds(halves[step] * per, per)].reshape(per * hd, 4 * rows)
        gpart[step] = jnp.dot(mat, cots[...], preferred_element_type=F32).astype(BF16).reshape(
            per, hd, half
        )
        for r in order(step):
            i = place(step, r)
            gy[step, r] = start(
                gpart.at[step, 2 * i + 1 - y], yrecv.at[step, i],
                gy_s.at[step, r], gy_r.at[step, r], (d, other),
            )

    def order(step):
        return list(range(nh)) if step == 0 else list(range(1, nh)) + [0]

    def place(step, r):
        return r if step == 0 else (z % nh + r) % nh

    def reduce(step, r):
        i = place(step, r)
        gy[step, r].wait_recv()
        pair = gpart[step, 2 * i + y].astype(F32) + yrecv[step, i].astype(F32)
        if step == 1 and r == 0:
            return pair
        to = halves[step] * nh + i
        j = (to - z + nz) % nz
        zsend[step, r] = pair.astype(BF16)
        start(zsend.at[step, r], zrecv.at[j], gz_s.at[step, r], gz_r.at[j], (d, 2 * to + y))

    todo = {(0, OPEN): [open_links]}
    for key, fn, arg in PLAN:
        todo.setdefault(key, []).append(functools.partial(
            {"send": send_chunk, "pass": pass_chunk, "w": pass_weight, "comb": combine,
             "grad": gradient}[fn], arg))
    for step in range(2):
        for h in range(2 * per):
            attend(step, h)
            for act in todo.get((step, h), []):
                act()
    for k in range(len(f_in), len(cuts) - 1):
        pass_chunk(k)
    for j in range(len(wy), nz):
        pass_weight(j)
    chunks = len(cuts) - 1
    if (0, 0) not in gy:
        for c_in in cot_in:
            c_in.wait_recv()
        for k in range(chunks // 2):
            combine(k)
        gradient(0)
    for k in range(chunks // 2, chunks):
        combine(k)
    gradient(1)
    for r in order(0):
        reduce(0, r)

    for made in wy:
        made.wait_recv()
    embs = []
    wmat = wq[...].reshape(half, half)
    for j in (2, 3, 1, 0):
        m = (d + j) % 4
        part = lax.dot_general(
            placed[:, :, block(m)].reshape(half, rows), wmat, (((0,), (0,)), ((), ())),
            preferred_element_type=F32,
        )
        if j == 0:
            eown[...] = part
        else:
            esend[j] = part.astype(BF16)
            embs.append(start(esend.at[j], ebuf.at[d], e_s.at[j], e_r.at[j], (m, f)))

    for r in order(1):
        own = reduce(1, r)
    for j in range(1, nz):
        copy(zsend.at[0, 0], zrecv.at[j], gz_s.at[0, 0], gz_r.at[j], (d, other)).wait_recv()
        own = own + zrecv[j].astype(F32)

    def turn_at(i):
        return turned.at[shard_half(i // 2), side(i % 2)]

    turned[shard_half(x), side(c)] = own.astype(BF16)
    t_in = [
        start(turn_at(d), turn_at(d), t_s.at[j], t_r.at[j], (m, f))
        for j, m in enumerate((across, partner))
    ]
    me = d * n_fs + f
    squares = own * own
    squares = jnp.sum(squares.reshape(hd // 8, 8, half), axis=0)
    srecv[me] = sum(squares[:, i:i + LANES] for i in range(0, half, LANES))
    s_in = []
    for i in range(4):
        for j in range(n_fs):
            if i or j:
                n = i * n_fs + j
                s_in.append(start(
                    srecv.at[me], srecv.at[me], q_s.at[n], q_r.at[n], ((d + i) % 4, (f + j) % n_fs)
                ))
    for made in embs:
        made.wait_recv()
    emb_ref[0, :, side(c)] = (eown[...] + ebuf[across].astype(F32)).astype(BF16)
    emb_ref[0, :, side(1 - c)] = (
        ebuf[partner].astype(F32) + ebuf[2 * (1 - x) + 1 - c].astype(F32)
    ).astype(BF16)
    t_in[0].wait_recv()
    t_in.append(start(turn_at(across), turn_at(across), t_s.at[2], t_r.at[2], (partner, f)))
    for made in s_in:
        made.wait_recv()
    norm = jnp.sqrt(jnp.sum(jnp.sum(srecv[...], axis=0), keepdims=True) + 1e-06)
    factor_ref[...] = jnp.broadcast_to(jnp.minimum(1.0, float(width) / norm), factor_ref.shape)
    for made in t_in[1:]:
        made.wait_recv()
    grad_ref[...] = turned[...]
    for made in sent:
        made.wait_send()


def settle(emb_ref, rows_ref, factor_ref, emb_out, grad_out):
    emb_out[...] = emb_ref[...]
    grad_out[...] = rows_ref[...].astype(F32) * factor_ref[0:1, 0:1]


def local(n_dp, n_fs, group, queries, keys, values, block_len, target, cotangent, out_weight):
    slots, rows, width = queries.shape
    shard = out_weight.shape[0]
    window, starts = starts_of(width, group)
    nz = n_fs // 2
    finish = group == n_dp
    vmem = pl.BlockSpec(memory_space=pltpu.VMEM)
    smem = pl.BlockSpec(memory_space=pltpu.SMEM)
    sem = lambda *shape: pltpu.SemaphoreType.DMA(shape)
    mates = max(group - 1, 1)
    parts = len(marks_of(width)) - 1
    embedding, rows_sum, factor = pl.pallas_call(
        functools.partial(kernel, n_dp, n_fs, group, finish),
        out_shape=(
            jax.ShapeDtypeStruct(cotangent.shape, BF16),
            jax.ShapeDtypeStruct((shard, width), BF16),
            jax.ShapeDtypeStruct((8, LANES), F32),
        ),
        in_specs=[smem, smem] + [vmem] * 5,
        out_specs=(vmem, vmem, vmem),
        scratch_shapes=[
            pltpu.VMEM((width, window), BF16),
            pltpu.VMEM((group * rows, window), BF16),
            pltpu.VMEM((rows, width), BF16),
            pltpu.VMEM((rows, width), BF16),
            pltpu.VMEM((rows, width), BF16),
            pltpu.VMEM((group * rows, width), BF16),
            pltpu.VMEM((width, window), BF16),
            pltpu.VMEM((nz, shard, window), BF16),
            pltpu.VMEM((nz, shard, window), BF16),
            pltpu.VMEM((nz, shard, window), BF16),
            pltpu.VMEM((group, rows, window), BF16),
            pltpu.VMEM((group, rows, window), BF16),
            pltpu.VMEM((group, shard, window), BF16),
            pltpu.VMEM((8, LANES), F32),
            pltpu.VMEM((n_fs, 8, LANES), F32),
            pltpu.VMEM((group, 8, LANES), F32),
            sem(nz), sem(nz), sem(nz), sem(nz), sem(mates), sem(mates), sem(parts), sem(parts),
            sem(parts, mates), sem(parts, mates), sem(nz), sem(nz), sem(nz), sem(nz),
            sem(mates), sem(mates), sem(mates), sem(mates), sem(n_fs), sem(n_fs),
            sem(mates), sem(mates),
        ],
        compiler_params=pltpu.CompilerParams(collective_id=0, has_side_effects=True),
    )(block_len, target, queries, keys, values, cotangent, out_weight)
    embedding, grad = pl.pallas_call(
        settle,
        out_shape=(
            jax.ShapeDtypeStruct(cotangent.shape, BF16),
            jax.ShapeDtypeStruct((shard, width), F32),
        ),
        in_specs=[vmem] * 3,
        out_specs=(vmem, vmem),
    )(embedding, rows_sum, factor)
    if not finish:
        lines = [[i for i in range(n_dp) if i % group == g] for g in range(group)]
        grad = lax.psum(grad, "dp", axis_index_groups=lines)
        squares = lax.psum(jnp.sum(grad * grad), "fsdp")
        grad = grad * jnp.minimum(1.0, float(width) / jnp.sqrt(squares + 1e-06))
    return embedding, grad


def local_quad(n_fs, queries, keys, values, block_len, target, cotangent, out_weight):
    slots, rows, width = queries.shape
    shard = out_weight.shape[0]
    hd, half, nz = width // HEADS, width // 2, n_fs // 2
    vmem = pl.BlockSpec(memory_space=pltpu.VMEM)
    smem = pl.BlockSpec(memory_space=pltpu.SMEM)
    sem = lambda *shape: pltpu.SemaphoreType.DMA(shape)
    buf = lambda *shape: pltpu.VMEM(shape, BF16)
    chunks = len(CUTS) - 1
    embedding, rows_sum, factor = pl.pallas_call(
        functools.partial(kernel_quad, n_fs),
        out_shape=(
            jax.ShapeDtypeStruct(cotangent.shape, BF16),
            jax.ShapeDtypeStruct((shard, width), BF16),
            jax.ShapeDtypeStruct((8, LANES), F32),
        ),
        in_specs=[smem, smem] + [vmem] * 5,
        out_specs=(vmem, vmem, vmem),
        scratch_shapes=[
            buf(2, 2, n_fs, hd, rows), buf(4, 2, n_fs, hd, rows), buf(n_fs, hd, 4 * rows),
            buf(4 * rows, half), buf(n_fs, hd, half), buf(2, nz, hd, half),
            buf(2, nz // 2, hd, half), buf(2, nz // 2, hd, half), buf(nz, hd, half),
            buf(4, rows, half), buf(4, rows, half), pltpu.VMEM((rows, half), F32),
            buf(shard, width), pltpu.VMEM((4 * n_fs, 8, LANES), F32),
            sem(nz), sem(nz), sem(nz), sem(nz), sem(4), sem(4),
            sem(chunks), sem(chunks), sem(chunks), sem(chunks), sem(chunks), sem(chunks),
            sem(2, nz // 2), sem(2, nz // 2), sem(2, nz // 2), sem(nz), sem(4), sem(4),
            sem(3), sem(3), sem(4 * n_fs), sem(4 * n_fs),
        ],
        compiler_params=pltpu.CompilerParams(collective_id=0, has_side_effects=True),
    )(block_len, target, queries, keys, values, cotangent, out_weight)
    return pl.pallas_call(
        settle,
        out_shape=(
            jax.ShapeDtypeStruct(cotangent.shape, BF16),
            jax.ShapeDtypeStruct((shard, width), F32),
        ),
        in_specs=[vmem] * 3,
        out_specs=(vmem, vmem),
    )(embedding, rows_sum, factor)


def solution(mesh):
    n_dp, n_fs = mesh.shape["dp"], mesh.shape["fsdp"]
    group = math.gcd(n_dp, 4)
    quad = n_dp == 4 and n_fs % 4 == 0 and HEADS == 2 * n_fs
    both = P(("dp", "fsdp"), None, None)
    flat = P(("dp", "fsdp"))
    return jax.shard_map(
        functools.partial(local_quad, n_fs) if quad else functools.partial(local, n_dp, n_fs, group),
        mesh=mesh,
        in_specs=(both, both, both, flat, flat, both, P("fsdp", None)),
        out_specs=(both, P("fsdp", None)),
        check_vma=False,
    )
```

```python
import functools
import math

import jax
import jax.numpy as jnp
from jax import lax
from jax.experimental import pallas as pl
from jax.experimental.pallas import tpu as pltpu
from jax.sharding import PartitionSpec as P

HEADS = 16
LANES = 128
MESH = pl.DeviceIdType.MESH
F32 = jnp.float32
BF16 = jnp.bfloat16


def starts_of(width, group):
    tiles = width // LANES
    window = -(-tiles // group) * LANES
    return window, [min(i * window, width - window) for i in range(group)]


def marks_of(width):
    tiles = width // LANES
    return [tiles * tenths // 10 * LANES for tenths in (0, 4, 7, 9, 10)]


def kernel(
    n_dp, n_fs, group, finish,
    len_ref, tgt_ref, q_ref, k_ref, v_ref, cot_ref, w_ref,
    emb_ref, grad_ref, factor_ref,
    wq, cq, mine, nxt, arr, placed, gpart, yrecv, zsend, zrecv, esend, ebuf, tbuf, sbuf, srecv, gsum,
    wz_s, wz_r, wy_s, wy_r, c_s, c_r, n_s, n_r, p_s, p_r, gy_s, gy_r, gz_s, gz_r,
    e_s, e_r, t_s, t_r, q_s, q_r, m_s, m_r,
):
    slots, rows, width = q_ref.shape
    shard = w_ref.shape[0]
    hd = width // HEADS
    window, starts = starts_of(width, group)
    over = group * window - width
    nz = n_fs // 2
    d, f = lax.axis_index("dp"), lax.axis_index("fsdp")
    base = (d // group) * group
    gi = d - base
    z, y = f // 2, f % 2
    other = z * 2 + (1 - y)
    ahead, behind = (d + 1) % n_dp, (d + n_dp - 1) % n_dp
    mates = [(gi + j) % group for j in range(1, group)]
    core, side = gi % 2, gi // 2
    partner, across = side * 2 + (1 - core), (1 - side) * 2 + core

    def start_of(i):
        if group == 1:
            return 0
        return pl.multiple_of(i * window - (i // (group - 1)) * over, LANES)

    def copy(src, dst, s, r, to):
        return pltpu.make_async_remote_copy(
            src_ref=src, dst_ref=dst, send_sem=s, recv_sem=r, device_id=to, device_id_type=MESH
        )

    def spread(at, s, r):
        to = [partner, across] if group == 4 else mates
        made = [copy(at(gi), at(gi), s(j), r(j), (base + m, f)) for j, m in enumerate(to)]
        for c in made:
            c.start()
        return made

    def relay(made, at, s, r):
        if group != 4:
            return made
        made[1].wait_recv()
        c = copy(at(across), at(across), s(2), r(2), (base + partner, f))
        c.start()
        made.append(c)
        return [made[0], c]

    barrier = pltpu.get_barrier_semaphore()
    peers = [(ahead, f), (behind, f)]
    peers += [(base + m, f) for m in mates]
    peers += [(d, (f + j) % n_fs) for j in range(1, n_fs)]
    for peer in peers:
        pl.semaphore_signal(barrier, inc=1, device_id=peer, device_id_type=MESH)

    my_cols = pl.ds(start_of(gi), window)
    my_rows = pl.ds(pl.multiple_of(gi * rows, rows), rows)

    def w_at(index):
        return wq.at[pl.ds(pl.multiple_of(index * shard, shard), shard), :]

    wz, wy, cots = [], [], []

    def open_links():
        pl.semaphore_wait(barrier, len(peers))
        w_src = w_ref.at[:, my_cols]
        for j in range(1, nz):
            c = copy(w_src, w_at(f), wz_s.at[j], wz_r.at[j], (d, ((z + j) % nz) * 2 + y))
            c.start()
            wz.append(c)
        wy.append(copy(w_src, w_at(f), wy_s.at[0], wy_r.at[0], (d, other)))
        wy[0].start()
        for j, m in enumerate(mates):
            c = copy(
                cot_ref.at[0, :, pl.ds(start_of(m), window)], cq.at[my_rows, :],
                c_s.at[j], c_r.at[j], (base + m, f),
            )
            c.start()
            cots.append(c)
        wq[pl.ds(pl.multiple_of(f * shard, shard), shard), :] = w_ref[:, my_cols]
        cq[my_rows, :] = cot_ref[0, :, my_cols]

    key_pos = lax.broadcasted_iota(jnp.int32, (rows, rows), 1)
    row_pos = lax.broadcasted_iota(jnp.int32, (rows, LANES), 0)
    lens = [len_ref[s] for s in range(slots)]
    usable = [key_pos < lens[s] for s in range(slots)]
    limit = [[jnp.where(tgt_ref[s] == t, lens[s], 0) for s in range(slots)] for t in range(2)]
    keep = [[row_pos < limit[t][s] for s in range(slots)] for t in range(2)]
    tiles = {}
    marks = marks_of(width)
    parts = len(marks) - 1
    nexts, cast_all = [], []

    def send_next(part):
        cols = pl.ds(marks[part], marks[part + 1] - marks[part])
        c = copy(nxt.at[:, cols], arr.at[:, cols], n_s.at[part], n_r.at[part], (ahead, f))
        c.start()
        nexts.append(c)

    def placed_at(part):
        cols = pl.ds(marks[part], marks[part + 1] - marks[part])
        return lambda i: placed.at[pl.ds(pl.multiple_of(i * rows, rows), rows), cols]

    def cast(part):
        nexts[part].wait_recv()
        cols = pl.ds(marks[part], marks[part + 1] - marks[part])
        placed[my_rows, cols] = mine[:, cols] + arr[:, cols]
        return spread(placed_at(part), lambda j: p_s.at[part, j], lambda j: p_r.at[part, j])

    def hand_on(part, made):
        return relay(
            made, placed_at(part), lambda j: p_s.at[part, j], lambda j: p_r.at[part, j]
        )

    for h in range(HEADS):
        first, last = h * hd, (h + 1) * hd
        lo, hi = first // LANES * LANES, -(-last // LANES) * LANES
        lane = lax.broadcasted_iota(jnp.int32, (rows, hi - lo), 1) + lo
        inside = (lane >= first) & (lane < last)
        for s in range(slots):
            query = jnp.where(inside, q_ref[s, :, lo:hi].astype(F32), 0.0).astype(BF16)
            scores = lax.dot_general(
                query, k_ref[s, :, lo:hi], (((1,), (1,)), ((), ())), preferred_element_type=F32
            ) * hd ** (-0.5)
            scores = jnp.where(usable[s], scores, -1e30)
            exponent = jnp.exp(scores - jnp.max(scores, axis=-1, keepdims=True))
            weights = (exponent / jnp.sum(exponent, axis=-1, keepdims=True)).astype(BF16)
            mixed = jnp.dot(weights, v_ref[s, :, lo:hi], preferred_element_type=F32)
            mixed = jnp.where(inside, mixed, 0.0)
            for t in range(lo // LANES, hi // LANES):
                piece = mixed[:, t * LANES - lo:(t + 1) * LANES - lo]
                tiles[s, t] = tiles[s, t] + piece if (s, t) in tiles else piece
        for t in range(lo // LANES, hi // LANES):
            if (t + 1) * LANES <= last:
                cols = slice(t * LANES, (t + 1) * LANES)
                for dest, ref in ((0, mine), (1, nxt)):
                    total = sum(
                        jnp.where(keep[dest][s], tiles[s, t], 0.0) for s in range(slots)
                    )
                    ref[:, cols] = total.astype(BF16)
        if h == HEADS // 8 - 1:
            open_links()
        ready = last // LANES * LANES
        while len(nexts) < parts - 1 and marks[len(nexts) + 1] <= ready:
            send_next(len(nexts))
            if len(nexts) > 1:
                cast_all.append(cast(len(nexts) - 2))
    send_next(parts - 1)
    cast_all.append(cast(parts - 2))
    waits = hand_on(0, cast_all[0])
    cast_all.append(cast(parts - 1))
    for j in range(1, nz):
        wz[j - 1].wait_recv()
        from_f = ((z + nz - j) % nz) * 2 + y
        c = copy(w_at(from_f), w_at(from_f), wy_s.at[j], wy_r.at[j], (d, other))
        c.start()
        wy.append(c)

    for part in range(1, parts):
        waits += hand_on(part, cast_all[part])
    casts = sum(cast_all, [])
    for c in cots + waits:
        c.wait_recv()

    step = 2 * LANES
    for i in range(width // step):
        gpart[i * step:(i + 1) * step, :] = lax.dot_general(
            placed[:, i * step:(i + 1) * step], cq[...], (((0,), (0,)), ((), ())),
            preferred_element_type=F32,
        ).astype(BF16)

    def g_rows(index):
        return pl.ds(pl.multiple_of(index * shard, shard), shard)

    order = list(range(1, nz)) + [0]
    gy = []
    for j in order:
        zj = (z + j) % nz
        c = copy(
            gpart.at[g_rows(zj * 2 + (1 - y)), :], yrecv.at[zj],
            gy_s.at[j], gy_r.at[j], (d, other),
        )
        c.start()
        gy.append(c)
    gz = []
    for j, c in zip(order, gy):
        zj = (z + j) % nz
        c.wait_recv()
        pair = gpart[g_rows(zj * 2 + y), :].astype(F32) + yrecv[zj].astype(F32)
        if j == 0:
            own = pair
        else:
            zsend[j] = pair.astype(BF16)
            c = copy(zsend.at[j], zrecv.at[j], gz_s.at[j], gz_r.at[j], (d, zj * 2 + y))
            c.start()
            gz.append(c)

    for c in wy:
        c.wait_recv()
    embs = []
    for i in range(group):
        esend[i] = jnp.dot(
            placed[i * rows:(i + 1) * rows, :], wq[...], preferred_element_type=F32
        ).astype(BF16)
    for j, m in enumerate(mates):
        c = copy(esend.at[m], ebuf.at[gi], e_s.at[j], e_r.at[j], (base + m, f))
        c.start()
        embs.append(c)
    ebuf[gi] = esend[gi]

    for c in gz:
        c.wait_recv()
    for j in range(1, nz):
        own = own + zrecv[j].astype(F32)
    ends = starts[1:] + [width]
    tbuf[gi] = own.astype(BF16)
    turn_at = lambda i: tbuf.at[i]
    turn_s, turn_r = (lambda j: t_s.at[j]), (lambda j: t_r.at[j])
    turns = spread(turn_at, turn_s, turn_r)
    squares = []
    if finish:
        valid = window
        for i in range(group):
            valid = jnp.where(gi == i, ends[i] - starts[i], valid)
        lane = lax.broadcasted_iota(jnp.int32, (8, LANES), 1)
        total = jnp.zeros((8, LANES), F32)
        for col in range(0, window, LANES):
            tile = own[:, col:col + LANES].astype(BF16).astype(F32)
            part = jnp.sum((tile * tile).reshape(shard // 8, 8, LANES), axis=0)
            total = total + jnp.where(lane + col < valid, part, 0.0)
        sbuf[...] = total
        for j in range(1, n_fs):
            c = copy(sbuf, srecv.at[j], q_s.at[j], q_r.at[j], (d, (f + j) % n_fs))
            c.start()
            squares.append(c)
    waits = relay(turns, turn_at, turn_s, turn_r)
    if finish:
        for j, c in zip(range(1, n_fs), squares):
            c.wait_recv()
            total = total + srecv[j]
        gsum[gi] = total
        for j, m in enumerate(mates):
            c = copy(gsum.at[gi], gsum.at[gi], m_s.at[j], m_r.at[j], (base + m, f))
            c.start()
            squares.append(c)
    for c in embs:
        c.wait_recv()
    for i in range(group):
        emb_ref[0, :, starts[i]:ends[i]] = ebuf[i, :, 0:ends[i] - starts[i]]
    for c in waits:
        c.wait_recv()
    if finish:
        for c in squares[n_fs - 1:]:
            c.wait_recv()
        total = gsum[0]
        for i in range(1, group):
            total = total + gsum[i]
        norm = jnp.sqrt(jnp.sum(total, keepdims=True) + 1e-06)
        factor = jnp.minimum(1.0, float(width) / norm)
    for i in range(group):
        grad_ref[:, starts[i]:ends[i]] = tbuf[i, :, 0:ends[i] - starts[i]]
    factor_ref[...] = jnp.broadcast_to(factor, factor_ref.shape) if finish else jnp.ones_like(factor_ref)
    for c in wz + wy + cots + nexts + casts + gy + gz + embs + turns + squares:
        c.wait_send()


CUTS = (0, 4, 8)
SPLIT = 256
DURING = {(0, 3): ("near", "cots0"), (0, 7): ("send0","cots1"), (1, 0): ("hop1",), (1, 7): ("send1",)}
AFTER = ("weight0", "hop2", "pass0", "comb0", "grad0", "weight1", "grad1", "red00", "red01", "weight2", "pass1", "comb1", "grad2", "red10", "red11", "emb", "red21")


def kernel_quad(
    n_fs,
    len_ref, tgt_ref, q_ref, k_ref, v_ref, cot_ref, w_ref,
    emb_ref, grad_ref, factor_ref,
    qv, kv, vv, att, got, placed, cots, wq, gpart, yrecv, zsend, zrecv, esend, ebuf, eown, turned, srecv,
    wz_s, wz_r, wy_s, wy_r, c_s, c_r, kc_s, kc_r, kx_s, kx_r, kf_s, kf_r,
    gy_s, gy_r, gz_s, gz_r, e_s, e_r, t_s, t_r, q_s, q_r, l_s, hop,
):
    slots, rows, width = q_ref.shape
    hd = width // HEADS
    half = width // 2
    nz = n_fs // 2
    nh = nz // 2
    per = n_fs // 2
    d, f = lax.axis_index("dp"), lax.axis_index("fsdp")
    x, c = d // 2, d % 2
    z, y = f // 2, f % 2
    partner, across = 2 * x + 1 - c, 2 * (1 - x) + c
    other = 2 * z + 1 - y
    halves = [1 - z // nh, z // nh]

    def copy(src, dst, s, r, to):
        return pltpu.make_async_remote_copy(
            src_ref=src, dst_ref=dst, send_sem=s, recv_sem=r, device_id=to, device_id_type=MESH
        )

    sent = []

    def start(*args):
        made = copy(*args)
        made.start()
        sent.append(made)
        return made

    barrier = pltpu.get_barrier_semaphore()
    up, down = z + 1 < nz, z > 0
    beside = up.astype(jnp.int32) + down.astype(jnp.int32)

    def both_sides(sem):
        @pl.when(up)
        def _():
            pl.semaphore_signal(sem, inc=1, device_id=(d, f + 2), device_id_type=MESH)

        @pl.when(down)
        def _():
            pl.semaphore_signal(sem, inc=1, device_id=(d, f - 2), device_id_type=MESH)

    peers = [((d + i) % 4, f) for i in range(1, 4)] + [(d, other)]
    for peer in peers:
        pl.semaphore_signal(barrier, inc=1, device_id=peer, device_id_type=MESH)
    both_sides(barrier)

    def side(i):
        return pl.ds(pl.multiple_of(i * half, LANES), half)

    def shard_half(i):
        return pl.ds(pl.multiple_of(i * hd, 16), hd)

    def block(i):
        return pl.ds(pl.multiple_of(i * rows, rows), rows)

    def load(src, dst, n):
        made = pltpu.make_async_copy(src, dst, l_s.at[n])
        made.start()
        return made

    loads = [
        [load(a.at[:, :, side(halves[t])], b.at[:, :, side(halves[t])], 3 * t + n)
         for n, (a, b) in enumerate(((q_ref, qv), (k_ref, kv), (v_ref, vv)))]
        for t in range(2)
    ]
    w_src = w_ref.at[shard_half(x), side(c)]
    own_in = [
        load(w_src, wq.at[f], 6),
        load(cot_ref.at[0, :, side(c)], cots.at[block(d), :], 7),
    ]

    wy, cot_in = [], []
    pieces = ((0, SPLIT), (SPLIT, half))
    low = z // nh

    def z_place(n):
        if n < nh - 1:
            return low * nh + (z % nh + 1 + n) % nh
        n = n - (nh - 1)
        return low * (nh - 1 - n) + (1 - low) * (nh + n)

    def send_weight(to, n):
        made = copy(w_src, wq.at[f], wz_s.at[n], wz_r.at[z], (d, to * 2 + y))
        made.start()

    def send_beside(way, there, n):
        @pl.when(there)
        def _():
            send_weight(z + way, n)

    def open_near():
        pl.semaphore_wait(barrier, len(peers) + beside)
        both_sides(hop.at[0])
        wy.append(start(w_src, wq.at[f], wy_s.at[0], wy_r.at[f], (d, other)))
        send_beside(1, up, 0)
        send_beside(-1, down, nz - 2)

    def open_far(n):
        pl.semaphore_wait(hop.at[n - 1], beside)
        if n < nz - 2:
            both_sides(hop.at[n])
        send_beside(n + 1, z + n + 1 < nz, n)
        send_beside(-n - 1, z > n, nz - 2 - n)

    def send_cots(p):
        a, b = pieces[p]
        for j in (2, 1, 3):
            m = (d + j) % 4
            at = pl.ds(pl.multiple_of((m % 2) * half + a, LANES), b - a)
            cot_in.append(start(
                cot_ref.at[0, :, at], cots.at[block(d), a:b], c_s.at[p, j], c_r.at[p, j], (m, f)
            ))

    def pass_weight(n):
        from_z = z_place(n)
        from_f = from_z * 2 + y
        copy(w_src, wq.at[from_f], wz_s.at[n], wz_r.at[from_z], (d, other)).wait_recv()
        wy.append(start(
            wq.at[from_f], wq.at[from_f], wy_s.at[n + 1], wy_r.at[from_f], (d, other)
        ))

    key_pos = lax.broadcasted_iota(jnp.int32, (rows, rows), 0)
    row_pos = lax.broadcasted_iota(jnp.int32, (hd, rows), 1)
    lens = [len_ref[s] for s in range(slots)]
    usable = [key_pos < lens[s] for s in range(slots)]
    keep = [
        [row_pos < jnp.where(tgt_ref[s] == t, lens[s], 0) for s in range(slots)] for t in range(2)
    ]
    scale = hd ** (-0.5) * math.log2(math.e)
    turned_v = {}

    def value_rows(step, s, first, last):
        found = []
        for t in range(first // LANES, -(-last // LANES)):
            if (step, s, t) not in turned_v:
                at = pl.ds(pl.multiple_of(halves[step] * half + t * LANES, LANES), LANES)
                turned_v[step, s, t] = vv[s, :, at].T
            a, b = max(first - t * LANES, 0), min(last - t * LANES, LANES)
            found.append(turned_v[step, s, t][a:b, :])
        return found[0] if len(found) == 1 else jnp.concatenate(found, axis=0)

    def attend(step, h):
        first, last = h * hd, (h + 1) * hd
        lo, hi = first // LANES * LANES, -(-last // LANES) * LANES
        at = pl.ds(pl.multiple_of(halves[step] * half + lo, LANES), hi - lo)
        lane = lax.broadcasted_iota(jnp.int32, (rows, hi - lo), 1) + lo
        inside = ((lane >= first) & (lane < last)).astype(F32).astype(BF16)
        mixed = []
        for s in range(slots):
            scores = lax.dot_general(
                kv[s, :, at], qv[s, :, at] * inside, (((1,), (1,)), ((), ())),
                preferred_element_type=F32,
            )
            scores = jnp.where(usable[s], scores, -1e30)
            exponent = jnp.exp2((scores - jnp.max(scores, axis=0, keepdims=True)) * scale)
            inverse = 1.0 / jnp.sum(exponent, axis=0, keepdims=True)
            weights = (exponent * inverse).astype(BF16)
            mixed.append(jnp.dot(
                value_rows(step, s, first, last), weights, preferred_element_type=F32
            ))
        for t in range(2):
            total = sum(jnp.where(keep[t][s], mixed[s], 0.0) for s in range(slots))
            att[t, h % 2, step * per + h // 2] = total.astype(BF16)

    cuts = CUTS
    core_in, x_in, f_in = [], [], []

    def send_chunk(k):
        a, n = cuts[k], cuts[k + 1] - cuts[k]
        at = pl.ds(a, n)
        core_in.append(start(
            att.at[:, x, at], got.at[d, :, at], kc_s.at[k], kc_r.at[k], (partner, f)
        ))
        x_in.append(start(
            att.at[:, 1 - x, at], got.at[d, :, at], kx_s.at[k], kx_r.at[k], (across, f)
        ))
        for t in range(2):
            got[d, t, at] = att[t, x, at]

    def pass_chunk(k):
        at = pl.ds(cuts[k], cuts[k + 1] - cuts[k])
        x_in[k].wait_recv()
        f_in.append(start(
            got.at[across, :, at], got.at[across, :, at], kf_s.at[k], kf_r.at[k], (partner, f)
        ))

    def combine(k):
        core_in[k].wait_recv()
        f_in[k].wait_recv()
        for s in range(cuts[k], cuts[k + 1]):
            index = halves[s // per] * per + s % per
            for b in range(4):
                placed[index, :, b * rows:(b + 1) * rows] = got[b, 0, s] + got[(b + 3) % 4, 1, s]

    gy = {}
    parts = [(0, *pieces[0]), (0, *pieces[1]), (1, 0, half)]

    def gradient(p):
        step, a, b = parts[p]
        mat = placed[pl.ds(halves[step] * per, per)].reshape(per * hd, 4 * rows)
        gpart[step, :, :, a:b] = jnp.dot(
            mat, cots[:, a:b], preferred_element_type=F32
        ).astype(BF16).reshape(per, hd, b - a)
        for r in order(step):
            i = place(step, r)
            gy[p, r] = start(
                gpart.at[step, 2 * i + 1 - y, :, a:b], yrecv.at[step, i, :, a:b],
                gy_s.at[p, r], gy_r.at[p, r], (d, other),
            )

    def order(step):
        return list(range(nh)) if step == 0 else list(range(1, nh)) + [0]

    def place(step, r):
        return r if step == 0 else (z % nh + r) % nh

    def reduce(p, r):
        step, a, b = parts[p]
        i = place(step, r)
        gy[p, r].wait_recv()
        pair = gpart[step, 2 * i + y, :, a:b].astype(F32) + yrecv[step, i, :, a:b].astype(F32)
        if step == 1 and r == 0:
            return pair
        to = halves[step] * nh + i
        j = (to - z + nz) % nz
        zsend[step, r, :, a:b] = pair.astype(BF16)
        start(
            zsend.at[step, r, :, a:b], zrecv.at[j, :, a:b], gz_s.at[p, r], gz_r.at[j],
            (d, 2 * to + y),
        )

    def gradient_in(p):
        if p < 2:
            for made in cot_in[3 * p:3 * p + 3]:
                made.wait_recv()
            if p == 0:
                own_in[1].wait()
        gradient(p)

    embs = []

    def embed():
        own_in[0].wait()
        for n in range(nz):
            from_z = z if n == nz - 1 else z_place(n)
            from_f = from_z * 2 + 1 - y
            copy(w_src, wq.at[from_f], wy_s.at[0], wy_r.at[from_f], (d, other)).wait_recv()
        wmat = wq[...].reshape(half, half)
        for j in (2, 3, 1, 0):
            m = (d + j) % 4
            part = lax.dot_general(
                placed[:, :, block(m)].reshape(half, rows), wmat, (((0,), (0,)), ((), ())),
                preferred_element_type=F32,
            )
            if j == 0:
                eown[...] = part
            else:
                esend[j] = part.astype(BF16)
                embs.append(start(esend.at[j], ebuf.at[d], e_s.at[j], e_r.at[j], (m, f)))

    acts = {"near": open_near, "emb": embed}
    for p in range(3):
        acts[f"grad{p}"] = functools.partial(gradient_in, p)
        for r in range(nh):
            acts[f"red{p}{r}"] = functools.partial(reduce, p, r)
    for p in range(2):
        acts[f"cots{p}"] = functools.partial(send_cots, p)
    for n in range(nz - 1):
        acts[f"weight{n}"] = functools.partial(pass_weight, n)
        acts[f"hop{n + 1}"] = functools.partial(open_far, n + 1)
    for k in range(len(cuts) - 1):
        acts[f"send{k}"] = functools.partial(send_chunk, k)
        acts[f"pass{k}"] = functools.partial(pass_chunk, k)
        acts[f"comb{k}"] = functools.partial(combine, k)

    for step in range(2):
        for made in loads[step]:
            made.wait()
        for h in range(2 * per):
            attend(step, h)
            for name in DURING.get((step, h), ()):
                acts[name]()
    for name in AFTER:
        acts[name]()

    own = reduce(2, 0)
    for j in range(1, nz):
        copy(zsend.at[0, 0], zrecv.at[j], gz_s.at[0, 0], gz_r.at[j], (d, other)).wait_recv()
        own = own + zrecv[j].astype(F32)

    def turn_at(i):
        return turned.at[shard_half(i // 2), side(i % 2)]

    turned[shard_half(x), side(c)] = own.astype(BF16)
    t_in = [
        start(turn_at(d), turn_at(d), t_s.at[j], t_r.at[j], (m, f))
        for j, m in enumerate((across, partner))
    ]
    me = d * n_fs + f
    squares = own * own
    squares = jnp.sum(squares.reshape(hd // 8, 8, half), axis=0)
    srecv[me] = sum(squares[:, i:i + LANES] for i in range(0, half, LANES))
    s_in = []
    for i in range(4):
        for j in range(n_fs):
            if i or j:
                n = i * n_fs + j
                s_in.append(start(
                    srecv.at[me], srecv.at[me], q_s.at[n], q_r.at[n], ((d + i) % 4, (f + j) % n_fs)
                ))
    for made in embs:
        made.wait_recv()
    emb_ref[0, :, side(c)] = (eown[...] + ebuf[across].astype(F32)).astype(BF16)
    emb_ref[0, :, side(1 - c)] = (
        ebuf[partner].astype(F32) + ebuf[2 * (1 - x) + 1 - c].astype(F32)
    ).astype(BF16)
    t_in[0].wait_recv()
    t_in.append(start(turn_at(across), turn_at(across), t_s.at[2], t_r.at[2], (partner, f)))
    for made in s_in:
        made.wait_recv()
    norm = jnp.sqrt(jnp.sum(jnp.sum(srecv[...], axis=0), keepdims=True) + 1e-06)
    factor_ref[...] = jnp.broadcast_to(jnp.minimum(1.0, float(width) / norm), factor_ref.shape)
    for made in t_in[1:]:
        made.wait_recv()
    grad_ref[...] = turned[...]
    for n in range(nz - 1):
        copy(w_src, wq.at[f], wz_s.at[n], wz_r.at[z], (d, other)).wait_send()
    for made in sent:
        made.wait_send()


def settle(emb_ref, rows_ref, factor_ref, emb_out, grad_out):
    emb_out[...] = emb_ref[...]
    grad_out[...] = rows_ref[...].astype(F32) * factor_ref[0:1, 0:1]


def local(n_dp, n_fs, group, queries, keys, values, block_len, target, cotangent, out_weight):
    slots, rows, width = queries.shape
    shard = out_weight.shape[0]
    window, starts = starts_of(width, group)
    nz = n_fs // 2
    finish = group == n_dp
    vmem = pl.BlockSpec(memory_space=pltpu.VMEM)
    smem = pl.BlockSpec(memory_space=pltpu.SMEM)
    sem = lambda *shape: pltpu.SemaphoreType.DMA(shape)
    mates = max(group - 1, 1)
    parts = len(marks_of(width)) - 1
    embedding, rows_sum, factor = pl.pallas_call(
        functools.partial(kernel, n_dp, n_fs, group, finish),
        out_shape=(
            jax.ShapeDtypeStruct(cotangent.shape, BF16),
            jax.ShapeDtypeStruct((shard, width), BF16),
            jax.ShapeDtypeStruct((8, LANES), F32),
        ),
        in_specs=[smem, smem] + [vmem] * 5,
        out_specs=(vmem, vmem, vmem),
        scratch_shapes=[
            pltpu.VMEM((width, window), BF16),
            pltpu.VMEM((group * rows, window), BF16),
            pltpu.VMEM((rows, width), BF16),
            pltpu.VMEM((rows, width), BF16),
            pltpu.VMEM((rows, width), BF16),
            pltpu.VMEM((group * rows, width), BF16),
            pltpu.VMEM((width, window), BF16),
            pltpu.VMEM((nz, shard, window), BF16),
            pltpu.VMEM((nz, shard, window), BF16),
            pltpu.VMEM((nz, shard, window), BF16),
            pltpu.VMEM((group, rows, window), BF16),
            pltpu.VMEM((group, rows, window), BF16),
            pltpu.VMEM((group, shard, window), BF16),
            pltpu.VMEM((8, LANES), F32),
            pltpu.VMEM((n_fs, 8, LANES), F32),
            pltpu.VMEM((group, 8, LANES), F32),
            sem(nz), sem(nz), sem(nz), sem(nz), sem(mates), sem(mates), sem(parts), sem(parts),
            sem(parts, mates), sem(parts, mates), sem(nz), sem(nz), sem(nz), sem(nz),
            sem(mates), sem(mates), sem(mates), sem(mates), sem(n_fs), sem(n_fs),
            sem(mates), sem(mates),
        ],
        compiler_params=pltpu.CompilerParams(collective_id=0, has_side_effects=True),
    )(block_len, target, queries, keys, values, cotangent, out_weight)
    embedding, grad = pl.pallas_call(
        settle,
        out_shape=(
            jax.ShapeDtypeStruct(cotangent.shape, BF16),
            jax.ShapeDtypeStruct((shard, width), F32),
        ),
        in_specs=[vmem] * 3,
        out_specs=(vmem, vmem),
    )(embedding, rows_sum, factor)
    if not finish:
        lines = [[i for i in range(n_dp) if i % group == g] for g in range(group)]
        grad = lax.psum(grad, "dp", axis_index_groups=lines)
        squares = lax.psum(jnp.sum(grad * grad), "fsdp")
        grad = grad * jnp.minimum(1.0, float(width) / jnp.sqrt(squares + 1e-06))
    return embedding, grad


def local_quad(n_fs, queries, keys, values, block_len, target, cotangent, out_weight):
    slots, rows, width = queries.shape
    shard = out_weight.shape[0]
    hd, half, nz = width // HEADS, width // 2, n_fs // 2
    vmem = pl.BlockSpec(memory_space=pltpu.VMEM)
    smem = pl.BlockSpec(memory_space=pltpu.SMEM)
    sem = lambda *shape: pltpu.SemaphoreType.DMA(shape)
    buf = lambda *shape: pltpu.VMEM(shape, BF16)
    chunks = len(CUTS) - 1
    embedding, rows_sum, factor = pl.pallas_call(
        functools.partial(kernel_quad, n_fs),
        out_shape=(
            jax.ShapeDtypeStruct(cotangent.shape, BF16),
            jax.ShapeDtypeStruct((shard, width), BF16),
            jax.ShapeDtypeStruct((8, LANES), F32),
        ),
        in_specs=[smem, smem] + [pl.BlockSpec(memory_space=pltpu.HBM)] * 5,
        out_specs=(vmem, vmem, vmem),
        scratch_shapes=[
            buf(slots, rows, width), buf(slots, rows, width), buf(slots, rows, width),
            buf(2, 2, n_fs, hd, rows), buf(4, 2, n_fs, hd, rows), buf(n_fs, hd, 4 * rows),
            buf(4 * rows, half), buf(n_fs, hd, half), buf(2, nz, hd, half),
            buf(2, nz // 2, hd, half), buf(2, nz // 2, hd, half), buf(nz, hd, half),
            buf(4, rows, half), buf(4, rows, half), pltpu.VMEM((rows, half), F32),
            buf(shard, width), pltpu.VMEM((4 * n_fs, 8, LANES), F32),
            sem(nz), sem(nz), sem(nz), sem(n_fs), sem(2, 4), sem(2, 4),
            sem(chunks), sem(chunks), sem(chunks), sem(chunks), sem(chunks), sem(chunks),
            sem(3, nz // 2), sem(3, nz // 2), sem(3, nz // 2), sem(nz), sem(4), sem(4),
            sem(3), sem(3), sem(4 * n_fs), sem(4 * n_fs), sem(8),
            pltpu.SemaphoreType.REGULAR((nz - 2,)),
        ],
        compiler_params=pltpu.CompilerParams(collective_id=0, has_side_effects=True),
    )(block_len, target, queries, keys, values, cotangent, out_weight)
    return pl.pallas_call(
        settle,
        out_shape=(
            jax.ShapeDtypeStruct(cotangent.shape, BF16),
            jax.ShapeDtypeStruct((shard, width), F32),
        ),
        in_specs=[vmem] * 3,
        out_specs=(vmem, vmem),
    )(embedding, rows_sum, factor)


def solution(mesh):
    n_dp, n_fs = mesh.shape["dp"], mesh.shape["fsdp"]
    group = math.gcd(n_dp, 4)
    quad = n_dp == 4 and n_fs % 4 == 0 and HEADS == 2 * n_fs
    both = P(("dp", "fsdp"), None, None)
    flat = P(("dp", "fsdp"))
    return jax.shard_map(
        functools.partial(local_quad, n_fs) if quad else functools.partial(local, n_dp, n_fs, group),
        mesh=mesh,
        in_specs=(both, both, both, flat, flat, both, P("fsdp", None)),
        out_specs=(both, P("fsdp", None)),
        check_vma=False,
    )
```

```python
import functools
import math

import jax
import jax.numpy as jnp
from jax import lax
from jax.experimental import pallas as pl
from jax.experimental.pallas import tpu as pltpu
from jax.sharding import PartitionSpec as P

HEADS = 16
LANES = 128
MESH = pl.DeviceIdType.MESH
F32 = jnp.float32
BF16 = jnp.bfloat16


def starts_of(width, group):
    tiles = width // LANES
    window = -(-tiles // group) * LANES
    return window, [min(i * window, width - window) for i in range(group)]


def marks_of(width):
    tiles = width // LANES
    return [tiles * tenths // 10 * LANES for tenths in (0, 4, 7, 9, 10)]


def kernel(
    n_dp, n_fs, group, finish,
    len_ref, tgt_ref, q_ref, k_ref, v_ref, cot_ref, w_ref,
    emb_ref, grad_ref, factor_ref,
    wq, cq, mine, nxt, arr, placed, gpart, yrecv, zsend, zrecv, esend, ebuf, tbuf, sbuf, srecv, gsum,
    wz_s, wz_r, wy_s, wy_r, c_s, c_r, n_s, n_r, p_s, p_r, gy_s, gy_r, gz_s, gz_r,
    e_s, e_r, t_s, t_r, q_s, q_r, m_s, m_r,
):
    slots, rows, width = q_ref.shape
    shard = w_ref.shape[0]
    hd = width // HEADS
    window, starts = starts_of(width, group)
    over = group * window - width
    nz = n_fs // 2
    d, f = lax.axis_index("dp"), lax.axis_index("fsdp")
    base = (d // group) * group
    gi = d - base
    z, y = f // 2, f % 2
    other = z * 2 + (1 - y)
    ahead, behind = (d + 1) % n_dp, (d + n_dp - 1) % n_dp
    mates = [(gi + j) % group for j in range(1, group)]
    core, side = gi % 2, gi // 2
    partner, across = side * 2 + (1 - core), (1 - side) * 2 + core

    def start_of(i):
        if group == 1:
            return 0
        return pl.multiple_of(i * window - (i // (group - 1)) * over, LANES)

    def copy(src, dst, s, r, to):
        return pltpu.make_async_remote_copy(
            src_ref=src, dst_ref=dst, send_sem=s, recv_sem=r, device_id=to, device_id_type=MESH
        )

    def spread(at, s, r):
        to = [partner, across] if group == 4 else mates
        made = [copy(at(gi), at(gi), s(j), r(j), (base + m, f)) for j, m in enumerate(to)]
        for c in made:
            c.start()
        return made

    def relay(made, at, s, r):
        if group != 4:
            return made
        made[1].wait_recv()
        c = copy(at(across), at(across), s(2), r(2), (base + partner, f))
        c.start()
        made.append(c)
        return [made[0], c]

    barrier = pltpu.get_barrier_semaphore()
    peers = [(ahead, f), (behind, f)]
    peers += [(base + m, f) for m in mates]
    peers += [(d, (f + j) % n_fs) for j in range(1, n_fs)]
    for peer in peers:
        pl.semaphore_signal(barrier, inc=1, device_id=peer, device_id_type=MESH)

    my_cols = pl.ds(start_of(gi), window)
    my_rows = pl.ds(pl.multiple_of(gi * rows, rows), rows)

    def w_at(index):
        return wq.at[pl.ds(pl.multiple_of(index * shard, shard), shard), :]

    wz, wy, cots = [], [], []

    def open_links():
        pl.semaphore_wait(barrier, len(peers))
        w_src = w_ref.at[:, my_cols]
        for j in range(1, nz):
            c = copy(w_src, w_at(f), wz_s.at[j], wz_r.at[j], (d, ((z + j) % nz) * 2 + y))
            c.start()
            wz.append(c)
        wy.append(copy(w_src, w_at(f), wy_s.at[0], wy_r.at[0], (d, other)))
        wy[0].start()
        for j, m in enumerate(mates):
            c = copy(
                cot_ref.at[0, :, pl.ds(start_of(m), window)], cq.at[my_rows, :],
                c_s.at[j], c_r.at[j], (base + m, f),
            )
            c.start()
            cots.append(c)
        wq[pl.ds(pl.multiple_of(f * shard, shard), shard), :] = w_ref[:, my_cols]
        cq[my_rows, :] = cot_ref[0, :, my_cols]

    key_pos = lax.broadcasted_iota(jnp.int32, (rows, rows), 1)
    row_pos = lax.broadcasted_iota(jnp.int32, (rows, LANES), 0)
    lens = [len_ref[s] for s in range(slots)]
    usable = [key_pos < lens[s] for s in range(slots)]
    limit = [[jnp.where(tgt_ref[s] == t, lens[s], 0) for s in range(slots)] for t in range(2)]
    keep = [[row_pos < limit[t][s] for s in range(slots)] for t in range(2)]
    tiles = {}
    marks = marks_of(width)
    parts = len(marks) - 1
    nexts, cast_all = [], []

    def send_next(part):
        cols = pl.ds(marks[part], marks[part + 1] - marks[part])
        c = copy(nxt.at[:, cols], arr.at[:, cols], n_s.at[part], n_r.at[part], (ahead, f))
        c.start()
        nexts.append(c)

    def placed_at(part):
        cols = pl.ds(marks[part], marks[part + 1] - marks[part])
        return lambda i: placed.at[pl.ds(pl.multiple_of(i * rows, rows), rows), cols]

    def cast(part):
        nexts[part].wait_recv()
        cols = pl.ds(marks[part], marks[part + 1] - marks[part])
        placed[my_rows, cols] = mine[:, cols] + arr[:, cols]
        return spread(placed_at(part), lambda j: p_s.at[part, j], lambda j: p_r.at[part, j])

    def hand_on(part, made):
        return relay(
            made, placed_at(part), lambda j: p_s.at[part, j], lambda j: p_r.at[part, j]
        )

    for h in range(HEADS):
        first, last = h * hd, (h + 1) * hd
        lo, hi = first // LANES * LANES, -(-last // LANES) * LANES
        lane = lax.broadcasted_iota(jnp.int32, (rows, hi - lo), 1) + lo
        inside = (lane >= first) & (lane < last)
        for s in range(slots):
            query = jnp.where(inside, q_ref[s, :, lo:hi].astype(F32), 0.0).astype(BF16)
            scores = lax.dot_general(
                query, k_ref[s, :, lo:hi], (((1,), (1,)), ((), ())), preferred_element_type=F32
            ) * hd ** (-0.5)
            scores = jnp.where(usable[s], scores, -1e30)
            exponent = jnp.exp(scores - jnp.max(scores, axis=-1, keepdims=True))
            weights = (exponent / jnp.sum(exponent, axis=-1, keepdims=True)).astype(BF16)
            mixed = jnp.dot(weights, v_ref[s, :, lo:hi], preferred_element_type=F32)
            mixed = jnp.where(inside, mixed, 0.0)
            for t in range(lo // LANES, hi // LANES):
                piece = mixed[:, t * LANES - lo:(t + 1) * LANES - lo]
                tiles[s, t] = tiles[s, t] + piece if (s, t) in tiles else piece
        for t in range(lo // LANES, hi // LANES):
            if (t + 1) * LANES <= last:
                cols = slice(t * LANES, (t + 1) * LANES)
                for dest, ref in ((0, mine), (1, nxt)):
                    total = sum(
                        jnp.where(keep[dest][s], tiles[s, t], 0.0) for s in range(slots)
                    )
                    ref[:, cols] = total.astype(BF16)
        if h == HEADS // 8 - 1:
            open_links()
        ready = last // LANES * LANES
        while len(nexts) < parts - 1 and marks[len(nexts) + 1] <= ready:
            send_next(len(nexts))
            if len(nexts) > 1:
                cast_all.append(cast(len(nexts) - 2))
    send_next(parts - 1)
    cast_all.append(cast(parts - 2))
    waits = hand_on(0, cast_all[0])
    cast_all.append(cast(parts - 1))
    for j in range(1, nz):
        wz[j - 1].wait_recv()
        from_f = ((z + nz - j) % nz) * 2 + y
        c = copy(w_at(from_f), w_at(from_f), wy_s.at[j], wy_r.at[j], (d, other))
        c.start()
        wy.append(c)

    for part in range(1, parts):
        waits += hand_on(part, cast_all[part])
    casts = sum(cast_all, [])
    for c in cots + waits:
        c.wait_recv()

    step = 2 * LANES
    for i in range(width // step):
        gpart[i * step:(i + 1) * step, :] = lax.dot_general(
            placed[:, i * step:(i + 1) * step], cq[...], (((0,), (0,)), ((), ())),
            preferred_element_type=F32,
        ).astype(BF16)

    def g_rows(index):
        return pl.ds(pl.multiple_of(index * shard, shard), shard)

    order = list(range(1, nz)) + [0]
    gy = []
    for j in order:
        zj = (z + j) % nz
        c = copy(
            gpart.at[g_rows(zj * 2 + (1 - y)), :], yrecv.at[zj],
            gy_s.at[j], gy_r.at[j], (d, other),
        )
        c.start()
        gy.append(c)
    gz = []
    for j, c in zip(order, gy):
        zj = (z + j) % nz
        c.wait_recv()
        pair = gpart[g_rows(zj * 2 + y), :].astype(F32) + yrecv[zj].astype(F32)
        if j == 0:
            own = pair
        else:
            zsend[j] = pair.astype(BF16)
            c = copy(zsend.at[j], zrecv.at[j], gz_s.at[j], gz_r.at[j], (d, zj * 2 + y))
            c.start()
            gz.append(c)

    for c in wy:
        c.wait_recv()
    embs = []
    for i in range(group):
        esend[i] = jnp.dot(
            placed[i * rows:(i + 1) * rows, :], wq[...], preferred_element_type=F32
        ).astype(BF16)
    for j, m in enumerate(mates):
        c = copy(esend.at[m], ebuf.at[gi], e_s.at[j], e_r.at[j], (base + m, f))
        c.start()
        embs.append(c)
    ebuf[gi] = esend[gi]

    for c in gz:
        c.wait_recv()
    for j in range(1, nz):
        own = own + zrecv[j].astype(F32)
    ends = starts[1:] + [width]
    tbuf[gi] = own.astype(BF16)
    turn_at = lambda i: tbuf.at[i]
    turn_s, turn_r = (lambda j: t_s.at[j]), (lambda j: t_r.at[j])
    turns = spread(turn_at, turn_s, turn_r)
    squares = []
    if finish:
        valid = window
        for i in range(group):
            valid = jnp.where(gi == i, ends[i] - starts[i], valid)
        lane = lax.broadcasted_iota(jnp.int32, (8, LANES), 1)
        total = jnp.zeros((8, LANES), F32)
        for col in range(0, window, LANES):
            tile = own[:, col:col + LANES].astype(BF16).astype(F32)
            part = jnp.sum((tile * tile).reshape(shard // 8, 8, LANES), axis=0)
            total = total + jnp.where(lane + col < valid, part, 0.0)
        sbuf[...] = total
        for j in range(1, n_fs):
            c = copy(sbuf, srecv.at[j], q_s.at[j], q_r.at[j], (d, (f + j) % n_fs))
            c.start()
            squares.append(c)
    waits = relay(turns, turn_at, turn_s, turn_r)
    if finish:
        for j, c in zip(range(1, n_fs), squares):
            c.wait_recv()
            total = total + srecv[j]
        gsum[gi] = total
        for j, m in enumerate(mates):
            c = copy(gsum.at[gi], gsum.at[gi], m_s.at[j], m_r.at[j], (base + m, f))
            c.start()
            squares.append(c)
    for c in embs:
        c.wait_recv()
    for i in range(group):
        emb_ref[0, :, starts[i]:ends[i]] = ebuf[i, :, 0:ends[i] - starts[i]]
    for c in waits:
        c.wait_recv()
    if finish:
        for c in squares[n_fs - 1:]:
            c.wait_recv()
        total = gsum[0]
        for i in range(1, group):
            total = total + gsum[i]
        norm = jnp.sqrt(jnp.sum(total, keepdims=True) + 1e-06)
        factor = jnp.minimum(1.0, float(width) / norm)
    for i in range(group):
        grad_ref[:, starts[i]:ends[i]] = tbuf[i, :, 0:ends[i] - starts[i]]
    factor_ref[...] = jnp.broadcast_to(factor, factor_ref.shape) if finish else jnp.ones_like(factor_ref)
    for c in wz + wy + cots + nexts + casts + gy + gz + embs + turns + squares:
        c.wait_send()


CUTS = (0, 4, 8)
SPLIT = 256
DURING = {(0, 3): ("near", "cots0"), (0, 7): ("send0","cots1"), (1, 0): ("hop1",), (1, 7): ("send1",)}
AFTER = ("weight0", "hop2", "pass0", "comb0", "grad0", "weight1", "grad1", "red00", "red01", "weight2", "pass1", "comb1", "grad2", "red10", "red11", "emb", "red21")


def kernel_quad(
    n_fs,
    len_ref, tgt_ref, q_ref, k_ref, v_ref, cot_ref, w_ref,
    emb_ref, grad_ref, factor_ref,
    qkv, att, got, placed, cots, wq, gpart, yrecv, zsend, zrecv, esend, ebuf, eown, turned, srecv,
    w_s, wz_r, wy_r, c_s, c_r, k_s, kx_r, kc_r, g_s, gy_r, gz_r, e_s, e_r, t_s, t_r, q_s, q_r,
    l_s, hop,
):
    slots, rows, width = q_ref.shape
    hd = width // HEADS
    half = width // 2
    nz = n_fs // 2
    nh = nz // 2
    per = n_fs // 2
    d, f = lax.axis_index("dp"), lax.axis_index("fsdp")
    x, c = d // 2, d % 2
    z, y = f // 2, f % 2
    partner, across = 2 * x + 1 - c, 2 * (1 - x) + c
    other = 2 * z + 1 - y
    halves = [1 - z // nh, z // nh]

    def copy(src, dst, s, r, to):
        return pltpu.make_async_remote_copy(
            src_ref=src, dst_ref=dst, send_sem=s, recv_sem=r, device_id=to, device_id_type=MESH
        )

    def start(*args):
        made = copy(*args)
        made.start()
        return made

    def landed(dst, r):
        copy(dst, dst, w_s, r, (d, f)).wait_recv()

    def left(src, s):
        copy(src, src, s, gz_r, (d, f)).wait_send()

    barrier = pltpu.get_barrier_semaphore()
    up, down = z + 1 < nz, z > 0
    beside = up.astype(jnp.int32) + down.astype(jnp.int32)

    def both_sides(sem):
        @pl.when(up)
        def _():
            pl.semaphore_signal(sem, inc=1, device_id=(d, f + 2), device_id_type=MESH)

        @pl.when(down)
        def _():
            pl.semaphore_signal(sem, inc=1, device_id=(d, f - 2), device_id_type=MESH)

    peers = [((d + i) % 4, f) for i in range(1, 4)] + [(d, other)]
    for peer in peers:
        pl.semaphore_signal(barrier, inc=1, device_id=peer, device_id_type=MESH)
    both_sides(barrier)

    def side(i):
        return pl.ds(pl.multiple_of(i * half, LANES), half)

    def shard_half(i):
        return pl.ds(pl.multiple_of(i * hd, 16), hd)

    def block(i):
        return pl.ds(pl.multiple_of(i * rows, rows), rows)

    for t in range(2):
        for n, ref in enumerate((q_ref, k_ref, v_ref)):
            at = side(halves[t])
            pltpu.make_async_copy(ref.at[:, :, at], qkv.at[n, :, :, at], l_s.at[t]).start()
    w_src = w_ref.at[shard_half(x), side(c)]
    own_w = pltpu.make_async_copy(w_src, wq.at[f], l_s.at[2])
    own_cot = pltpu.make_async_copy(cot_ref.at[0, :, side(c)], cots.at[block(d), :], l_s.at[3])
    own_w.start()
    own_cot.start()

    pieces = ((0, SPLIT), (SPLIT, half))
    low = z // nh

    def z_place(n):
        if n < nh - 1:
            return low * nh + (z % nh + 1 + n) % nh
        n = n - (nh - 1)
        return low * (nh - 1 - n) + (1 - low) * (nh + n)

    def send_beside(way, there):
        @pl.when(there)
        def _():
            start(w_src, wq.at[f], w_s, wz_r.at[z], (d, (z + way) * 2 + y))

    def open_near():
        pl.semaphore_wait(barrier, len(peers) + beside)
        both_sides(hop.at[0])
        start(w_src, wq.at[f], w_s, wy_r, (d, other))
        send_beside(1, up)
        send_beside(-1, down)

    def open_far(n):
        pl.semaphore_wait(hop.at[n - 1], beside)
        if n < nz - 2:
            both_sides(hop.at[n])
        send_beside(n + 1, z + n + 1 < nz)
        send_beside(-n - 1, z > n)

    def send_cots(p):
        a, b = pieces[p]
        for j in (2, 1, 3):
            m = (d + j) % 4
            at = pl.ds(pl.multiple_of((m % 2) * half + a, LANES), b - a)
            start(cot_ref.at[0, :, at], cots.at[block(d), a:b], c_s, c_r.at[p], (m, f))

    def pass_weight(n):
        from_z = z_place(n)
        here = wq.at[from_z * 2 + y]
        landed(here, wz_r.at[from_z])
        start(here, here, w_s, wy_r, (d, other))

    key_pos = lax.broadcasted_iota(jnp.int32, (rows, rows), 0)
    row_pos = lax.broadcasted_iota(jnp.int32, (hd, rows), 1)
    lens = [len_ref[s] for s in range(slots)]
    usable = [key_pos < lens[s] for s in range(slots)]
    keep = [
        [row_pos < jnp.where(tgt_ref[s] == t, lens[s], 0) for s in range(slots)] for t in range(2)
    ]
    scale = hd ** (-0.5) * math.log2(math.e)
    turned_v = {}

    def value_rows(step, s, first, last):
        found = []
        for t in range(first // LANES, -(-last // LANES)):
            if (step, s, t) not in turned_v:
                at = pl.ds(pl.multiple_of(halves[step] * half + t * LANES, LANES), LANES)
                turned_v[step, s, t] = qkv[2, s, :, at].T
            a, b = max(first - t * LANES, 0), min(last - t * LANES, LANES)
            found.append(turned_v[step, s, t][a:b, :])
        return found[0] if len(found) == 1 else jnp.concatenate(found, axis=0)

    def attend(step, h):
        first, last = h * hd, (h + 1) * hd
        lo, hi = first // LANES * LANES, -(-last // LANES) * LANES
        at = pl.ds(pl.multiple_of(halves[step] * half + lo, LANES), hi - lo)
        lane = lax.broadcasted_iota(jnp.int32, (rows, hi - lo), 1) + lo
        inside = ((lane >= first) & (lane < last)).astype(F32).astype(BF16)
        mixed = []
        for s in range(slots):
            scores = lax.dot_general(
                qkv[1, s, :, at], qkv[0, s, :, at] * inside, (((1,), (1,)), ((), ())),
                preferred_element_type=F32,
            )
            scores = jnp.where(usable[s], scores, -1e30)
            exponent = jnp.exp2((scores - jnp.max(scores, axis=0, keepdims=True)) * scale)
            inverse = 1.0 / jnp.sum(exponent, axis=0, keepdims=True)
            weights = (exponent * inverse).astype(BF16)
            mixed.append(jnp.dot(
                value_rows(step, s, first, last), weights, preferred_element_type=F32
            ))
        for t in range(2):
            total = sum(jnp.where(keep[t][s], mixed[s], 0.0) for s in range(slots))
            att[t, h % 2, step * per + h // 2] = total.astype(BF16)

    cuts = CUTS

    def send_chunk(k):
        at = pl.ds(cuts[k], cuts[k + 1] - cuts[k])
        start(att.at[:, 1 - x, at], got.at[d, :, at], k_s, kx_r.at[k], (across, f))
        start(att.at[:, x, at], got.at[d, :, at], k_s, kc_r.at[k], (partner, f))
        for t in range(2):
            got[d, t, at] = att[t, x, at]

    def pass_chunk(k):
        here = got.at[across, :, pl.ds(cuts[k], cuts[k + 1] - cuts[k])]
        landed(here, kx_r.at[k])
        start(here, here, k_s, kc_r.at[k], (partner, f))

    def combine(k):
        landed(got.at[0:2, :, pl.ds(cuts[k], cuts[k + 1] - cuts[k])], kc_r.at[k])
        for s in range(cuts[k], cuts[k + 1]):
            index = halves[s // per] * per + s % per
            for b in range(4):
                placed[index, :, b * rows:(b + 1) * rows] = got[b, 0, s] + got[(b + 3) % 4, 1, s]

    gy = {}
    parts = [(0, *pieces[0]), (0, *pieces[1]), (1, 0, half)]

    def gradient(p):
        step, a, b = parts[p]
        mat = placed[pl.ds(halves[step] * per, per)].reshape(per * hd, 4 * rows)
        gpart[step, :, :, a:b] = jnp.dot(
            mat, cots[:, a:b], preferred_element_type=F32
        ).astype(BF16).reshape(per, hd, b - a)
        for r in order(step):
            i = place(step, r)
            gy[p, r] = start(
                gpart.at[step, 2 * i + 1 - y, :, a:b], yrecv.at[step, i, :, a:b],
                g_s, gy_r.at[p, r], (d, other),
            )

    def order(step):
        return list(range(nh)) if step == 0 else list(range(1, nh)) + [0]

    def place(step, r):
        return r if step == 0 else (z % nh + r) % nh

    def reduce(p, r):
        step, a, b = parts[p]
        i = place(step, r)
        gy[p, r].wait_recv()
        pair = gpart[step, 2 * i + y, :, a:b].astype(F32) + yrecv[step, i, :, a:b].astype(F32)
        if step == 1 and r == 0:
            return pair
        to = halves[step] * nh + i
        j = (to - z + nz) % nz
        zsend[step, r, :, a:b] = pair.astype(BF16)
        start(
            zsend.at[step, r, :, a:b], zrecv.at[j, :, a:b], g_s, gz_r, (d, 2 * to + y),
        )

    def gradient_in(p):
        if p < 2:
            a, b = pieces[p]
            landed(cots.at[0:3 * rows, a:b], c_r.at[p])
            if p == 0:
                own_cot.wait()
        gradient(p)

    def embed():
        own_w.wait()
        landed(wq.at[0:nz], wy_r)
        wmat = wq[...].reshape(half, half)
        for j in (2, 3, 1, 0):
            m = (d + j) % 4
            part = lax.dot_general(
                placed[:, :, block(m)].reshape(half, rows), wmat, (((0,), (0,)), ((), ())),
                preferred_element_type=F32,
            )
            if j == 0:
                eown[...] = part
            else:
                esend[j] = part.astype(BF16)
                start(esend.at[j], ebuf.at[d], e_s, e_r, (m, f))

    acts = {"near": open_near, "emb": embed}
    for p in range(3):
        acts[f"grad{p}"] = functools.partial(gradient_in, p)
        for r in range(nh):
            acts[f"red{p}{r}"] = functools.partial(reduce, p, r)
    for p in range(2):
        acts[f"cots{p}"] = functools.partial(send_cots, p)
    for n in range(nz - 1):
        acts[f"weight{n}"] = functools.partial(pass_weight, n)
        acts[f"hop{n + 1}"] = functools.partial(open_far, n + 1)
    for k in range(len(cuts) - 1):
        acts[f"send{k}"] = functools.partial(send_chunk, k)
        acts[f"pass{k}"] = functools.partial(pass_chunk, k)
        acts[f"comb{k}"] = functools.partial(combine, k)

    for step in range(2):
        here = qkv.at[:, :, :, 0:half]
        pltpu.make_async_copy(here, here, l_s.at[step]).wait()
        for h in range(2 * per):
            attend(step, h)
            for name in DURING.get((step, h), ()):
                acts[name]()
    for name in AFTER:
        acts[name]()

    own = reduce(2, 0)
    landed(zrecv.at[0:nz - 1], gz_r)
    for j in range(1, nz):
        own = own + zrecv[j].astype(F32)

    def turn_at(i):
        return turned.at[shard_half(i // 2), side(i % 2)]

    turned[shard_half(x), side(c)] = own.astype(BF16)
    for j, m in enumerate((across, partner)):
        start(turn_at(d), turn_at(d), t_s, t_r.at[j], (m, f))
    me = d * n_fs + f
    squares = jnp.sum((own * own).reshape(hd // 8, 8, half), axis=0)
    srecv[me] = sum(squares[:, i:i + LANES] for i in range(0, half, LANES))
    for n in reversed(range(-1, nz - 1)):
        to = z_place(n) if n >= 0 else z
        for k in range(1 if n < 0 else 0, 8):
            start(srecv.at[me], srecv.at[me], q_s, q_r, ((d + k // 2) % 4, 2 * to + (y + k) % 2))
    landed(esend.at[0:3], e_r)
    emb_ref[0, :, side(c)] = (eown[...] + ebuf[across].astype(F32)).astype(BF16)
    emb_ref[0, :, side(1 - c)] = (
        ebuf[partner].astype(F32) + ebuf[2 * (1 - x) + 1 - c].astype(F32)
    ).astype(BF16)
    landed(turn_at(across), t_r.at[0])
    start(turn_at(across), turn_at(across), t_s, t_r.at[1], (partner, f))
    landed(wq.at[0:2], t_r.at[1])
    grad_ref[...] = turned[...]
    landed(srecv.at[0:4 * n_fs - 1], q_r)
    norm = jnp.sqrt(jnp.sum(jnp.sum(srecv[...], axis=0), keepdims=True) + 1e-06)
    factor_ref[...] = jnp.broadcast_to(jnp.minimum(1.0, float(width) / norm), factor_ref.shape)
    left(wq.at[0:2 * nz - 1], w_s)
    left(cots.at[0:3 * rows], c_s)
    left(got.at[0:3], k_s)
    left(wq.at[0:2 * nz - 1], g_s)
    left(esend.at[0:3], e_s)
    left(wq.at[0:3], t_s)
    left(srecv.at[0:4 * n_fs - 1], q_s)


def settle(emb_ref, rows_ref, factor_ref, emb_out, grad_out):
    emb_out[...] = emb_ref[...]
    grad_out[...] = rows_ref[...].astype(F32) * factor_ref[0:1, 0:1]


def local(n_dp, n_fs, group, queries, keys, values, block_len, target, cotangent, out_weight):
    slots, rows, width = queries.shape
    shard = out_weight.shape[0]
    window, starts = starts_of(width, group)
    nz = n_fs // 2
    finish = group == n_dp
    vmem = pl.BlockSpec(memory_space=pltpu.VMEM)
    smem = pl.BlockSpec(memory_space=pltpu.SMEM)
    sem = lambda *shape: pltpu.SemaphoreType.DMA(shape)
    mates = max(group - 1, 1)
    parts = len(marks_of(width)) - 1
    embedding, rows_sum, factor = pl.pallas_call(
        functools.partial(kernel, n_dp, n_fs, group, finish),
        out_shape=(
            jax.ShapeDtypeStruct(cotangent.shape, BF16),
            jax.ShapeDtypeStruct((shard, width), BF16),
            jax.ShapeDtypeStruct((8, LANES), F32),
        ),
        in_specs=[smem, smem] + [vmem] * 5,
        out_specs=(vmem, vmem, vmem),
        scratch_shapes=[
            pltpu.VMEM((width, window), BF16),
            pltpu.VMEM((group * rows, window), BF16),
            pltpu.VMEM((rows, width), BF16),
            pltpu.VMEM((rows, width), BF16),
            pltpu.VMEM((rows, width), BF16),
            pltpu.VMEM((group * rows, width), BF16),
            pltpu.VMEM((width, window), BF16),
            pltpu.VMEM((nz, shard, window), BF16),
            pltpu.VMEM((nz, shard, window), BF16),
            pltpu.VMEM((nz, shard, window), BF16),
            pltpu.VMEM((group, rows, window), BF16),
            pltpu.VMEM((group, rows, window), BF16),
            pltpu.VMEM((group, shard, window), BF16),
            pltpu.VMEM((8, LANES), F32),
            pltpu.VMEM((n_fs, 8, LANES), F32),
            pltpu.VMEM((group, 8, LANES), F32),
            sem(nz), sem(nz), sem(nz), sem(nz), sem(mates), sem(mates), sem(parts), sem(parts),
            sem(parts, mates), sem(parts, mates), sem(nz), sem(nz), sem(nz), sem(nz),
            sem(mates), sem(mates), sem(mates), sem(mates), sem(n_fs), sem(n_fs),
            sem(mates), sem(mates),
        ],
        compiler_params=pltpu.CompilerParams(collective_id=0, has_side_effects=True),
    )(block_len, target, queries, keys, values, cotangent, out_weight)
    embedding, grad = pl.pallas_call(
        settle,
        out_shape=(
            jax.ShapeDtypeStruct(cotangent.shape, BF16),
            jax.ShapeDtypeStruct((shard, width), F32),
        ),
        in_specs=[vmem] * 3,
        out_specs=(vmem, vmem),
    )(embedding, rows_sum, factor)
    if not finish:
        lines = [[i for i in range(n_dp) if i % group == g] for g in range(group)]
        grad = lax.psum(grad, "dp", axis_index_groups=lines)
        squares = lax.psum(jnp.sum(grad * grad), "fsdp")
        grad = grad * jnp.minimum(1.0, float(width) / jnp.sqrt(squares + 1e-06))
    return embedding, grad


def local_quad(n_fs, queries, keys, values, block_len, target, cotangent, out_weight):
    slots, rows, width = queries.shape
    shard = out_weight.shape[0]
    hd, half, nz = width // HEADS, width // 2, n_fs // 2
    vmem = pl.BlockSpec(memory_space=pltpu.VMEM)
    smem = pl.BlockSpec(memory_space=pltpu.SMEM)
    sem = lambda *shape: pltpu.SemaphoreType.DMA(shape)
    one = pltpu.SemaphoreType.DMA
    buf = lambda *shape: pltpu.VMEM(shape, BF16)
    chunks = len(CUTS) - 1
    embedding, rows_sum, factor = pl.pallas_call(
        functools.partial(kernel_quad, n_fs),
        out_shape=(
            jax.ShapeDtypeStruct(cotangent.shape, BF16),
            jax.ShapeDtypeStruct((shard, width), BF16),
            jax.ShapeDtypeStruct((8, LANES), F32),
        ),
        in_specs=[smem, smem] + [pl.BlockSpec(memory_space=pltpu.HBM)] * 5,
        out_specs=(vmem, vmem, vmem),
        scratch_shapes=[
            buf(3, slots, rows, width),
            buf(2, 2, n_fs, hd, rows), buf(4, 2, n_fs, hd, rows), buf(n_fs, hd, 4 * rows),
            buf(4 * rows, half), buf(n_fs, hd, half), buf(2, nz, hd, half),
            buf(2, nz // 2, hd, half), buf(2, nz // 2, hd, half), buf(nz, hd, half),
            buf(4, rows, half), buf(4, rows, half), pltpu.VMEM((rows, half), F32),
            buf(shard, width), pltpu.VMEM((4 * n_fs, 8, LANES), F32),
            one, sem(nz), one, one, sem(2), one, sem(chunks), sem(chunks), one, sem(3, nz // 2), one,
            one, one, one, sem(2), one, one, sem(4), pltpu.SemaphoreType.REGULAR((nz - 2,)),
        ],
        compiler_params=pltpu.CompilerParams(collective_id=0, has_side_effects=True),
    )(block_len, target, queries, keys, values, cotangent, out_weight)
    return pl.pallas_call(
        settle,
        out_shape=(
            jax.ShapeDtypeStruct(cotangent.shape, BF16),
            jax.ShapeDtypeStruct((shard, width), F32),
        ),
        in_specs=[vmem] * 3,
        out_specs=(vmem, vmem),
    )(embedding, rows_sum, factor)


def solution(mesh):
    n_dp, n_fs = mesh.shape["dp"], mesh.shape["fsdp"]
    group = math.gcd(n_dp, 4)
    quad = n_dp == 4 and n_fs % 4 == 0 and HEADS == 2 * n_fs
    both = P(("dp", "fsdp"), None, None)
    flat = P(("dp", "fsdp"))
    return jax.shard_map(
        functools.partial(local_quad, n_fs) if quad else functools.partial(local, n_dp, n_fs, group),
        mesh=mesh,
        in_specs=(both, both, both, flat, flat, both, P("fsdp", None)),
        out_specs=(both, P("fsdp", None)),
        check_vma=False,
    )
```

```python
import functools
import math

import jax
import jax.numpy as jnp
from jax import lax
from jax.experimental import pallas as pl
from jax.experimental.pallas import tpu as pltpu
from jax.sharding import PartitionSpec as P

HEADS = 16
LANES = 128
MESH = pl.DeviceIdType.MESH
F32 = jnp.float32
BF16 = jnp.bfloat16


def starts_of(width, group):
    tiles = width // LANES
    window = -(-tiles // group) * LANES
    return window, [min(i * window, width - window) for i in range(group)]


def marks_of(width):
    tiles = width // LANES
    return [tiles * tenths // 10 * LANES for tenths in (0, 4, 7, 9, 10)]


def kernel(
    n_dp, n_fs, group, finish,
    len_ref, tgt_ref, q_ref, k_ref, v_ref, cot_ref, w_ref,
    emb_ref, grad_ref, factor_ref,
    wq, cq, mine, nxt, arr, placed, gpart, yrecv, zsend, zrecv, esend, ebuf, tbuf, sbuf, srecv, gsum,
    wz_s, wz_r, wy_s, wy_r, c_s, c_r, n_s, n_r, p_s, p_r, gy_s, gy_r, gz_s, gz_r,
    e_s, e_r, t_s, t_r, q_s, q_r, m_s, m_r,
):
    slots, rows, width = q_ref.shape
    shard = w_ref.shape[0]
    hd = width // HEADS
    window, starts = starts_of(width, group)
    over = group * window - width
    nz = n_fs // 2
    d, f = lax.axis_index("dp"), lax.axis_index("fsdp")
    base = (d // group) * group
    gi = d - base
    z, y = f // 2, f % 2
    other = z * 2 + (1 - y)
    ahead, behind = (d + 1) % n_dp, (d + n_dp - 1) % n_dp
    mates = [(gi + j) % group for j in range(1, group)]
    core, side = gi % 2, gi // 2
    partner, across = side * 2 + (1 - core), (1 - side) * 2 + core

    def start_of(i):
        if group == 1:
            return 0
        return pl.multiple_of(i * window - (i // (group - 1)) * over, LANES)

    def copy(src, dst, s, r, to):
        return pltpu.make_async_remote_copy(
            src_ref=src, dst_ref=dst, send_sem=s, recv_sem=r, device_id=to, device_id_type=MESH
        )

    def spread(at, s, r):
        to = [partner, across] if group == 4 else mates
        made = [copy(at(gi), at(gi), s(j), r(j), (base + m, f)) for j, m in enumerate(to)]
        for c in made:
            c.start()
        return made

    def relay(made, at, s, r):
        if group != 4:
            return made
        made[1].wait_recv()
        c = copy(at(across), at(across), s(2), r(2), (base + partner, f))
        c.start()
        made.append(c)
        return [made[0], c]

    barrier = pltpu.get_barrier_semaphore()
    peers = [(ahead, f), (behind, f)]
    peers += [(base + m, f) for m in mates]
    peers += [(d, (f + j) % n_fs) for j in range(1, n_fs)]
    for peer in peers:
        pl.semaphore_signal(barrier, inc=1, device_id=peer, device_id_type=MESH)

    my_cols = pl.ds(start_of(gi), window)
    my_rows = pl.ds(pl.multiple_of(gi * rows, rows), rows)

    def w_at(index):
        return wq.at[pl.ds(pl.multiple_of(index * shard, shard), shard), :]

    wz, wy, cots = [], [], []

    def open_links():
        pl.semaphore_wait(barrier, len(peers))
        w_src = w_ref.at[:, my_cols]
        for j in range(1, nz):
            c = copy(w_src, w_at(f), wz_s.at[j], wz_r.at[j], (d, ((z + j) % nz) * 2 + y))
            c.start()
            wz.append(c)
        wy.append(copy(w_src, w_at(f), wy_s.at[0], wy_r.at[0], (d, other)))
        wy[0].start()
        for j, m in enumerate(mates):
            c = copy(
                cot_ref.at[0, :, pl.ds(start_of(m), window)], cq.at[my_rows, :],
                c_s.at[j], c_r.at[j], (base + m, f),
            )
            c.start()
            cots.append(c)
        wq[pl.ds(pl.multiple_of(f * shard, shard), shard), :] = w_ref[:, my_cols]
        cq[my_rows, :] = cot_ref[0, :, my_cols]

    key_pos = lax.broadcasted_iota(jnp.int32, (rows, rows), 1)
    row_pos = lax.broadcasted_iota(jnp.int32, (rows, LANES), 0)
    lens = [len_ref[s] for s in range(slots)]
    usable = [key_pos < lens[s] for s in range(slots)]
    limit = [[jnp.where(tgt_ref[s] == t, lens[s], 0) for s in range(slots)] for t in range(2)]
    keep = [[row_pos < limit[t][s] for s in range(slots)] for t in range(2)]
    tiles = {}
    marks = marks_of(width)
    parts = len(marks) - 1
    nexts, cast_all = [], []

    def send_next(part):
        cols = pl.ds(marks[part], marks[part + 1] - marks[part])
        c = copy(nxt.at[:, cols], arr.at[:, cols], n_s.at[part], n_r.at[part], (ahead, f))
        c.start()
        nexts.append(c)

    def placed_at(part):
        cols = pl.ds(marks[part], marks[part + 1] - marks[part])
        return lambda i: placed.at[pl.ds(pl.multiple_of(i * rows, rows), rows), cols]

    def cast(part):
        nexts[part].wait_recv()
        cols = pl.ds(marks[part], marks[part + 1] - marks[part])
        placed[my_rows, cols] = mine[:, cols] + arr[:, cols]
        return spread(placed_at(part), lambda j: p_s.at[part, j], lambda j: p_r.at[part, j])

    def hand_on(part, made):
        return relay(
            made, placed_at(part), lambda j: p_s.at[part, j], lambda j: p_r.at[part, j]
        )

    for h in range(HEADS):
        first, last = h * hd, (h + 1) * hd
        lo, hi = first // LANES * LANES, -(-last // LANES) * LANES
        lane = lax.broadcasted_iota(jnp.int32, (rows, hi - lo), 1) + lo
        inside = (lane >= first) & (lane < last)
        for s in range(slots):
            query = jnp.where(inside, q_ref[s, :, lo:hi].astype(F32), 0.0).astype(BF16)
            scores = lax.dot_general(
                query, k_ref[s, :, lo:hi], (((1,), (1,)), ((), ())), preferred_element_type=F32
            ) * hd ** (-0.5)
            scores = jnp.where(usable[s], scores, -1e30)
            exponent = jnp.exp(scores - jnp.max(scores, axis=-1, keepdims=True))
            weights = (exponent / jnp.sum(exponent, axis=-1, keepdims=True)).astype(BF16)
            mixed = jnp.dot(weights, v_ref[s, :, lo:hi], preferred_element_type=F32)
            mixed = jnp.where(inside, mixed, 0.0)
            for t in range(lo // LANES, hi // LANES):
                piece = mixed[:, t * LANES - lo:(t + 1) * LANES - lo]
                tiles[s, t] = tiles[s, t] + piece if (s, t) in tiles else piece
        for t in range(lo // LANES, hi // LANES):
            if (t + 1) * LANES <= last:
                cols = slice(t * LANES, (t + 1) * LANES)
                for dest, ref in ((0, mine), (1, nxt)):
                    total = sum(
                        jnp.where(keep[dest][s], tiles[s, t], 0.0) for s in range(slots)
                    )
                    ref[:, cols] = total.astype(BF16)
        if h == HEADS // 8 - 1:
            open_links()
        ready = last // LANES * LANES
        while len(nexts) < parts - 1 and marks[len(nexts) + 1] <= ready:
            send_next(len(nexts))
            if len(nexts) > 1:
                cast_all.append(cast(len(nexts) - 2))
    send_next(parts - 1)
    cast_all.append(cast(parts - 2))
    waits = hand_on(0, cast_all[0])
    cast_all.append(cast(parts - 1))
    for j in range(1, nz):
        wz[j - 1].wait_recv()
        from_f = ((z + nz - j) % nz) * 2 + y
        c = copy(w_at(from_f), w_at(from_f), wy_s.at[j], wy_r.at[j], (d, other))
        c.start()
        wy.append(c)

    for part in range(1, parts):
        waits += hand_on(part, cast_all[part])
    casts = sum(cast_all, [])
    for c in cots + waits:
        c.wait_recv()

    step = 2 * LANES
    for i in range(width // step):
        gpart[i * step:(i + 1) * step, :] = lax.dot_general(
            placed[:, i * step:(i + 1) * step], cq[...], (((0,), (0,)), ((), ())),
            preferred_element_type=F32,
        ).astype(BF16)

    def g_rows(index):
        return pl.ds(pl.multiple_of(index * shard, shard), shard)

    order = list(range(1, nz)) + [0]
    gy = []
    for j in order:
        zj = (z + j) % nz
        c = copy(
            gpart.at[g_rows(zj * 2 + (1 - y)), :], yrecv.at[zj],
            gy_s.at[j], gy_r.at[j], (d, other),
        )
        c.start()
        gy.append(c)
    gz = []
    for j, c in zip(order, gy):
        zj = (z + j) % nz
        c.wait_recv()
        pair = gpart[g_rows(zj * 2 + y), :].astype(F32) + yrecv[zj].astype(F32)
        if j == 0:
            own = pair
        else:
            zsend[j] = pair.astype(BF16)
            c = copy(zsend.at[j], zrecv.at[j], gz_s.at[j], gz_r.at[j], (d, zj * 2 + y))
            c.start()
            gz.append(c)

    for c in wy:
        c.wait_recv()
    embs = []
    for i in range(group):
        esend[i] = jnp.dot(
            placed[i * rows:(i + 1) * rows, :], wq[...], preferred_element_type=F32
        ).astype(BF16)
    for j, m in enumerate(mates):
        c = copy(esend.at[m], ebuf.at[gi], e_s.at[j], e_r.at[j], (base + m, f))
        c.start()
        embs.append(c)
    ebuf[gi] = esend[gi]

    for c in gz:
        c.wait_recv()
    for j in range(1, nz):
        own = own + zrecv[j].astype(F32)
    ends = starts[1:] + [width]
    tbuf[gi] = own.astype(BF16)
    turn_at = lambda i: tbuf.at[i]
    turn_s, turn_r = (lambda j: t_s.at[j]), (lambda j: t_r.at[j])
    turns = spread(turn_at, turn_s, turn_r)
    squares = []
    if finish:
        valid = window
        for i in range(group):
            valid = jnp.where(gi == i, ends[i] - starts[i], valid)
        lane = lax.broadcasted_iota(jnp.int32, (8, LANES), 1)
        total = jnp.zeros((8, LANES), F32)
        for col in range(0, window, LANES):
            tile = own[:, col:col + LANES].astype(BF16).astype(F32)
            part = jnp.sum((tile * tile).reshape(shard // 8, 8, LANES), axis=0)
            total = total + jnp.where(lane + col < valid, part, 0.0)
        sbuf[...] = total
        for j in range(1, n_fs):
            c = copy(sbuf, srecv.at[j], q_s.at[j], q_r.at[j], (d, (f + j) % n_fs))
            c.start()
            squares.append(c)
    waits = relay(turns, turn_at, turn_s, turn_r)
    if finish:
        for j, c in zip(range(1, n_fs), squares):
            c.wait_recv()
            total = total + srecv[j]
        gsum[gi] = total
        for j, m in enumerate(mates):
            c = copy(gsum.at[gi], gsum.at[gi], m_s.at[j], m_r.at[j], (base + m, f))
            c.start()
            squares.append(c)
    for c in embs:
        c.wait_recv()
    for i in range(group):
        emb_ref[0, :, starts[i]:ends[i]] = ebuf[i, :, 0:ends[i] - starts[i]]
    for c in waits:
        c.wait_recv()
    if finish:
        for c in squares[n_fs - 1:]:
            c.wait_recv()
        total = gsum[0]
        for i in range(1, group):
            total = total + gsum[i]
        norm = jnp.sqrt(jnp.sum(total, keepdims=True) + 1e-06)
        factor = jnp.minimum(1.0, float(width) / norm)
    for i in range(group):
        grad_ref[:, starts[i]:ends[i]] = tbuf[i, :, 0:ends[i] - starts[i]]
    factor_ref[...] = jnp.broadcast_to(factor, factor_ref.shape) if finish else jnp.ones_like(factor_ref)
    for c in wz + wy + cots + nexts + casts + gy + gz + embs + turns + squares:
        c.wait_send()


CUTS = (0, 4, 8)
SPLIT = 256
DURING = {
    (0, 3): ("near", "cots0"), (0, 7): ("send0",), (1, 0): ("hop1",), (1, 3): ("join0", "cots1"),
    (1, 7): ("send1",),
}
AFTER = (
    "weight0", "hop2", "join1", "pass0", "more0", "comb0", "grad0", "weight1", "grad1",
    "red00", "red01", "weight2", "pass1", "more1", "comb1", "grad2", "grad3", "red10", "red11",
    "emb", "red21", "red31", "done0", "done1", "turn0", "turn1",
)


def kernel_quad(
    n_fs,
    len_ref, tgt_ref, q_ref, k_ref, v_ref, cot_ref, w_ref,
    emb_ref, grad_ref, factor_ref,
    qkv, att, got, placed, cots, wq, gpart, yrecv, zsend, zrecv, esend, ebuf, eown, turned, srecv,
    joined, w_s, wz_r, wy_r, c_s, c_r, k_s, f_s, kx_r, ks_r, kc_r, kf_r, j_r, g_s, gy_r, gz_r, e_s, e_r, t_s, t_r, q_s, q_r,
    l_s, hop,
):
    slots, rows, width = q_ref.shape
    hd = width // HEADS
    half = width // 2
    nz = n_fs // 2
    nh = nz // 2
    per = n_fs // 2
    d, f = lax.axis_index("dp"), lax.axis_index("fsdp")
    x, c = d // 2, d % 2
    z, y = f // 2, f % 2
    partner, across = 2 * x + 1 - c, 2 * (1 - x) + c
    other = 2 * z + 1 - y
    halves = [1 - z // nh, z // nh]

    def copy(src, dst, s, r, to):
        return pltpu.make_async_remote_copy(
            src_ref=src, dst_ref=dst, send_sem=s, recv_sem=r, device_id=to, device_id_type=MESH
        )

    def start(*args):
        made = copy(*args)
        made.start()
        return made

    def landed(dst, r):
        copy(dst, dst, w_s, r, (d, f)).wait_recv()

    def left(src, s):
        copy(src, src, s, wy_r, (d, f)).wait_send()

    barrier = pltpu.get_barrier_semaphore()
    up, down = z + 1 < nz, z > 0
    beside = up.astype(jnp.int32) + down.astype(jnp.int32)

    def both_sides(sem):
        @pl.when(up)
        def _():
            pl.semaphore_signal(sem, inc=1, device_id=(d, f + 2), device_id_type=MESH)

        @pl.when(down)
        def _():
            pl.semaphore_signal(sem, inc=1, device_id=(d, f - 2), device_id_type=MESH)

    peers = [((d + i) % 4, f) for i in range(1, 4)] + [(d, other)]
    for peer in peers:
        pl.semaphore_signal(barrier, inc=1, device_id=peer, device_id_type=MESH)
    both_sides(barrier)

    def side(i):
        return pl.ds(pl.multiple_of(i * half, LANES), half)

    def shard_half(i):
        return pl.ds(pl.multiple_of(i * hd, 16), hd)

    def block(i):
        return pl.ds(pl.multiple_of(i * rows, rows), rows)

    for t in range(2):
        for n, ref in enumerate((q_ref, k_ref, v_ref)):
            at = side(halves[t])
            pltpu.make_async_copy(ref.at[:, :, at], qkv.at[n, :, :, at], l_s.at[t]).start()
    w_src = w_ref.at[shard_half(x), side(c)]
    own_w = pltpu.make_async_copy(w_src, wq.at[f], l_s.at[2])
    own_cot = pltpu.make_async_copy(cot_ref.at[0, :, side(c)], cots.at[block(d), :], l_s.at[3])
    own_w.start()
    own_cot.start()

    pieces = ((0, SPLIT), (SPLIT, half))
    low = z // nh

    def z_place(n):
        if n < nh - 1:
            return low * nh + (z % nh + 1 + n) % nh
        n = n - (nh - 1)
        return low * (nh - 1 - n) + (1 - low) * (nh + n)

    def send_beside(way, there):
        @pl.when(there)
        def _():
            start(w_src, wq.at[f], w_s, wz_r.at[z], (d, (z + way) * 2 + y))

    def open_near():
        pl.semaphore_wait(barrier, len(peers) + beside)
        both_sides(hop.at[0])
        start(w_src, wq.at[f], w_s, wy_r, (d, other))
        send_beside(1, up)
        send_beside(-1, down)

    def open_far(n):
        pl.semaphore_wait(hop.at[n - 1], beside)
        if n < nz - 2:
            both_sides(hop.at[n])
        send_beside(n + 1, z + n + 1 < nz)
        send_beside(-n - 1, z > n)

    def send_cots(p):
        a, b = pieces[p]
        for j in (2, 1, 3):
            m = (d + j) % 4
            at = pl.ds(pl.multiple_of((m % 2) * half + a, LANES), b - a)
            start(cot_ref.at[0, :, at], cots.at[block(d), a:b], c_s, c_r.at[p], (m, f))

    def pass_weight(n):
        from_z = z_place(n)
        here = wq.at[from_z * 2 + y]
        landed(here, wz_r.at[from_z])
        start(here, here, w_s, wy_r, (d, other))

    key_pos = lax.broadcasted_iota(jnp.int32, (rows, rows), 0)
    row_pos = lax.broadcasted_iota(jnp.int32, (hd, rows), 1)
    lens = [len_ref[s] for s in range(slots)]
    usable = [key_pos < lens[s] for s in range(slots)]
    keep = [
        [row_pos < jnp.where(tgt_ref[s] == t, lens[s], 0) for s in range(slots)] for t in range(2)
    ]
    scale = hd ** (-0.5) * math.log2(math.e)
    turned_v = {}

    def value_rows(step, s, first, last):
        found = []
        for t in range(first // LANES, -(-last // LANES)):
            if (step, s, t) not in turned_v:
                at = pl.ds(pl.multiple_of(halves[step] * half + t * LANES, LANES), LANES)
                turned_v[step, s, t] = qkv[2, s, :, at].T
            a, b = max(first - t * LANES, 0), min(last - t * LANES, LANES)
            found.append(turned_v[step, s, t][a:b, :])
        return found[0] if len(found) == 1 else jnp.concatenate(found, axis=0)

    def attend(step, h):
        first, last = h * hd, (h + 1) * hd
        lo, hi = first // LANES * LANES, -(-last // LANES) * LANES
        at = pl.ds(pl.multiple_of(halves[step] * half + lo, LANES), hi - lo)
        lane = lax.broadcasted_iota(jnp.int32, (rows, hi - lo), 1) + lo
        inside = ((lane >= first) & (lane < last)).astype(F32).astype(BF16)
        mixed = []
        for s in range(slots):
            scores = lax.dot_general(
                qkv[1, s, :, at], qkv[0, s, :, at] * inside, (((1,), (1,)), ((), ())),
                preferred_element_type=F32,
            )
            scores = jnp.where(usable[s], scores, -1e30)
            exponent = jnp.exp2((scores - jnp.max(scores, axis=0, keepdims=True)) * scale)
            inverse = 1.0 / jnp.sum(exponent, axis=0, keepdims=True)
            weights = (exponent * inverse).astype(BF16)
            mixed.append(jnp.dot(
                value_rows(step, s, first, last), weights, preferred_element_type=F32
            ))
        for t in range(2):
            total = sum(jnp.where(keep[t][s], mixed[s], 0.0) for s in range(slots))
            att[t, h % 2, step * per + h // 2] = total.astype(BF16)

    cuts = CUTS

    def part_of(k, i):
        n = (cuts[k + 1] - cuts[k]) // 2
        return pl.ds(cuts[k] + i * n, n)

    def send_chunk(k):
        at = pl.ds(cuts[k], cuts[k + 1] - cuts[k])
        start(att.at[c, 1 - x, at], got.at[d, c, at], k_s, kx_r.at[k], (across, f))
        theirs = part_of(k, 1 - c)
        start(att.at[1 - c, 1 - x, theirs], joined.at[theirs], f_s, j_r.at[k], (partner, f))
        start(att.at[:, x, at], got.at[d, :, at], k_s, kc_r.at[k], (partner, f))
        for t in range(2):
            got[d, t, at] = att[t, x, at]

    def join_chunk(k):
        ours = part_of(k, c)
        landed(joined.at[ours], j_r.at[k])
        joined[ours] = joined[ours] + att[1 - c, 1 - x, ours]
        start(joined.at[ours], got.at[2 * x + 1, 0, ours], f_s, ks_r.at[k], (across, f))

    def pass_chunk(k):
        here = got.at[across, c, pl.ds(cuts[k], cuts[k + 1] - cuts[k])]
        landed(here, kx_r.at[k])
        start(here, here, f_s, kf_r.at[k], (partner, f))

    def pass_joined(k):
        here = got.at[2 * (1 - x) + 1, 0, part_of(k, c)]
        landed(here, ks_r.at[k])
        start(here, here, f_s, kf_r.at[k], (partner, f))

    def combine(k):
        n = cuts[k + 1] - cuts[k]
        landed(got.at[0, :, 0:n], kc_r.at[k])
        landed(got.at[0, 0, 0:n + n // 2], kf_r.at[k])
        for s in range(cuts[k], cuts[k + 1]):
            index = halves[s // per] * per + s % per
            for b in range(4):
                placed[index, :, b * rows:(b + 1) * rows] = got[b, 0, s] + got[(b + 3) % 4, 1, s]

    gy = {}
    parts = [(step, *piece) for step in range(2) for piece in pieces]

    def gradient(p):
        step, a, b = parts[p]
        mat = placed[pl.ds(halves[step] * per, per)].reshape(per * hd, 4 * rows)
        gpart[step, :, :, a:b] = jnp.dot(
            mat, cots[:, a:b], preferred_element_type=F32
        ).astype(BF16).reshape(per, hd, b - a)
        for r in order(step):
            if step == 0 or r:
                trade(p, r)

    def trade(p, r):
        step, a, b = parts[p]
        i = place(step, r)
        gy[p, r] = start(
            gpart.at[step, 2 * i + 1 - y, :, a:b], yrecv.at[step, i, :, a:b],
            g_s, gy_r.at[p, r], (d, other),
        )

    def order(step):
        return list(range(nh)) if step == 0 else list(range(1, nh)) + [0]

    def place(step, r):
        return r if step == 0 else (z % nh + r) % nh

    def reduce(p, r):
        step, a, b = parts[p]
        i = place(step, r)
        gy[p, r].wait_recv()
        pair = gpart[step, 2 * i + y, :, a:b].astype(F32) + yrecv[step, i, :, a:b].astype(F32)
        if step == 1 and r == 0:
            return pair
        to = halves[step] * nh + i
        j = (to - z + nz) % nz
        zsend[step, r, :, a:b] = pair.astype(BF16)
        start(
            zsend.at[step, r, :, a:b], zrecv.at[j, :, a:b], g_s, gz_r.at[p % 2], (d, 2 * to + y),
        )

    def gradient_in(p):
        if p < 2:
            a, b = pieces[p]
            landed(cots.at[0:3 * rows, a:b], c_r.at[p])
            if p == 0:
                own_cot.wait()
        gradient(p)
        if p == 3:
            trade(2, 0)
            trade(3, 0)

    def embed():
        own_w.wait()
        landed(wq.at[0:nz], wy_r)
        wmat = wq[...].reshape(half, half)
        for j in (2, 3, 1, 0):
            m = (d + j) % 4
            part = lax.dot_general(
                placed[:, :, block(m)].reshape(half, rows), wmat, (((0,), (0,)), ((), ())),
                preferred_element_type=F32,
            )
            if j == 0:
                eown[...] = part
            else:
                esend[j] = part.astype(BF16)
                start(esend.at[j], ebuf.at[d], e_s, e_r, (m, f))

    def turn_at(i, q):
        a, b = pieces[q]
        at = pl.ds(pl.multiple_of((i % 2) * half + a, LANES), b - a)
        return turned.at[shard_half(i // 2), at]

    me = d * n_fs + f
    squares = []

    def finish(q):
        a, b = pieces[q]
        own = reduce(2 + q, 0)
        landed(zrecv.at[0:nz - 1, :, a:b], gz_r.at[q])
        for j in range(1, nz):
            own = own + zrecv[j, :, a:b].astype(F32)
        turn_at(d, q)[...] = own.astype(BF16)
        start(turn_at(d, q), turn_at(d, q), t_s, t_r.at[q], (across, f))
        start(turn_at(d, q), turn_at(d, q), t_s, t_r.at[2], (partner, f))
        square = jnp.sum(own * own, axis=0, keepdims=True)
        squares.extend(square[:, i:i + LANES] for i in range(0, b - a, LANES))
        if b == half:
            srecv[me] = sum(squares)
            for n in reversed(range(-1, nz - 1)):
                to = z_place(n) if n >= 0 else z
                for k in range(1 if n < 0 else 0, 8):
                    peer = ((d + k // 2) % 4, 2 * to + (y + k) % 2)
                    start(srecv.at[me], srecv.at[me], q_s, q_r, peer)

    def pass_turn(q):
        landed(turn_at(across, q), t_r.at[q])
        start(turn_at(across, q), turn_at(across, q), t_s, t_r.at[2], (partner, f))

    acts = {"near": open_near, "emb": embed}
    for p in range(4):
        acts[f"grad{p}"] = functools.partial(gradient_in, p)
        for r in range(nh):
            acts[f"red{p}{r}"] = functools.partial(reduce, p, r)
    for p in range(2):
        acts[f"cots{p}"] = functools.partial(send_cots, p)
        acts[f"done{p}"] = functools.partial(finish, p)
        acts[f"turn{p}"] = functools.partial(pass_turn, p)
    for n in range(nz - 1):
        acts[f"weight{n}"] = functools.partial(pass_weight, n)
        acts[f"hop{n + 1}"] = functools.partial(open_far, n + 1)
    for k in range(len(cuts) - 1):
        acts[f"send{k}"] = functools.partial(send_chunk, k)
        acts[f"join{k}"] = functools.partial(join_chunk, k)
        acts[f"pass{k}"] = functools.partial(pass_chunk, k)
        acts[f"more{k}"] = functools.partial(pass_joined, k)
        acts[f"comb{k}"] = functools.partial(combine, k)

    got[2 * (1 - x), 1] = jnp.zeros_like(got[0, 0])
    for step in range(2):
        here = qkv.at[:, :, :, 0:half]
        pltpu.make_async_copy(here, here, l_s.at[step]).wait()
        for h in range(2 * per):
            attend(step, h)
            for name in DURING.get((step, h), ()):
                acts[name]()
    for name in AFTER:
        acts[name]()

    landed(esend.at[0:3], e_r)
    emb_ref[0, :, side(c)] = (eown[...] + ebuf[across].astype(F32)).astype(BF16)
    emb_ref[0, :, side(1 - c)] = (
        ebuf[partner].astype(F32) + ebuf[2 * (1 - x) + 1 - c].astype(F32)
    ).astype(BF16)
    landed(wq.at[0:2], t_r.at[2])
    grad_ref[...] = turned[...]
    landed(srecv.at[0:4 * n_fs - 1], q_r)
    norm = jnp.sqrt(jnp.sum(jnp.sum(srecv[...], axis=0), keepdims=True) + 1e-06)
    factor_ref[...] = jnp.broadcast_to(jnp.minimum(1.0, float(width) / norm), factor_ref.shape)
    left(wq.at[0:2 * nz - 1], w_s)
    left(cots.at[0:3 * rows], c_s)
    left(got.at[0:3, 0], k_s)
    left(got.at[0:2, :, 0:n_fs * 5 // 8], f_s)
    left(wq.at[0:2 * nz - 1], g_s)
    left(esend.at[0:3], e_s)
    left(wq.at[0:3], t_s)
    left(srecv.at[0:4 * n_fs - 1], q_s)


def settle(emb_ref, rows_ref, factor_ref, emb_out, grad_out):
    emb_out[...] = emb_ref[...]
    grad_out[...] = rows_ref[...].astype(F32) * factor_ref[0:1, 0:1]


def local(n_dp, n_fs, group, queries, keys, values, block_len, target, cotangent, out_weight):
    slots, rows, width = queries.shape
    shard = out_weight.shape[0]
    window, starts = starts_of(width, group)
    nz = n_fs // 2
    finish = group == n_dp
    vmem = pl.BlockSpec(memory_space=pltpu.VMEM)
    smem = pl.BlockSpec(memory_space=pltpu.SMEM)
    sem = lambda *shape: pltpu.SemaphoreType.DMA(shape)
    mates = max(group - 1, 1)
    parts = len(marks_of(width)) - 1
    embedding, rows_sum, factor = pl.pallas_call(
        functools.partial(kernel, n_dp, n_fs, group, finish),
        out_shape=(
            jax.ShapeDtypeStruct(cotangent.shape, BF16),
            jax.ShapeDtypeStruct((shard, width), BF16),
            jax.ShapeDtypeStruct((8, LANES), F32),
        ),
        in_specs=[smem, smem] + [vmem] * 5,
        out_specs=(vmem, vmem, vmem),
        scratch_shapes=[
            pltpu.VMEM((width, window), BF16),
            pltpu.VMEM((group * rows, window), BF16),
            pltpu.VMEM((rows, width), BF16),
            pltpu.VMEM((rows, width), BF16),
            pltpu.VMEM((rows, width), BF16),
            pltpu.VMEM((group * rows, width), BF16),
            pltpu.VMEM((width, window), BF16),
            pltpu.VMEM((nz, shard, window), BF16),
            pltpu.VMEM((nz, shard, window), BF16),
            pltpu.VMEM((nz, shard, window), BF16),
            pltpu.VMEM((group, rows, window), BF16),
            pltpu.VMEM((group, rows, window), BF16),
            pltpu.VMEM((group, shard, window), BF16),
            pltpu.VMEM((8, LANES), F32),
            pltpu.VMEM((n_fs, 8, LANES), F32),
            pltpu.VMEM((group, 8, LANES), F32),
            sem(nz), sem(nz), sem(nz), sem(nz), sem(mates), sem(mates), sem(parts), sem(parts),
            sem(parts, mates), sem(parts, mates), sem(nz), sem(nz), sem(nz), sem(nz),
            sem(mates), sem(mates), sem(mates), sem(mates), sem(n_fs), sem(n_fs),
            sem(mates), sem(mates),
        ],
        compiler_params=pltpu.CompilerParams(collective_id=0, has_side_effects=True),
    )(block_len, target, queries, keys, values, cotangent, out_weight)
    embedding, grad = pl.pallas_call(
        settle,
        out_shape=(
            jax.ShapeDtypeStruct(cotangent.shape, BF16),
            jax.ShapeDtypeStruct((shard, width), F32),
        ),
        in_specs=[vmem] * 3,
        out_specs=(vmem, vmem),
    )(embedding, rows_sum, factor)
    if not finish:
        lines = [[i for i in range(n_dp) if i % group == g] for g in range(group)]
        grad = lax.psum(grad, "dp", axis_index_groups=lines)
        squares = lax.psum(jnp.sum(grad * grad), "fsdp")
        grad = grad * jnp.minimum(1.0, float(width) / jnp.sqrt(squares + 1e-06))
    return embedding, grad


def local_quad(n_fs, queries, keys, values, block_len, target, cotangent, out_weight):
    slots, rows, width = queries.shape
    shard = out_weight.shape[0]
    hd, half, nz = width // HEADS, width // 2, n_fs // 2
    vmem = pl.BlockSpec(memory_space=pltpu.VMEM)
    smem = pl.BlockSpec(memory_space=pltpu.SMEM)
    sem = lambda *shape: pltpu.SemaphoreType.DMA(shape)
    one = pltpu.SemaphoreType.DMA
    buf = lambda *shape: pltpu.VMEM(shape, BF16)
    chunks = len(CUTS) - 1
    embedding, rows_sum, factor = pl.pallas_call(
        functools.partial(kernel_quad, n_fs),
        out_shape=(
            jax.ShapeDtypeStruct(cotangent.shape, BF16),
            jax.ShapeDtypeStruct((shard, width), BF16),
            jax.ShapeDtypeStruct((8, LANES), F32),
        ),
        in_specs=[smem, smem] + [pl.BlockSpec(memory_space=pltpu.HBM)] * 5,
        out_specs=(vmem, vmem, vmem),
        scratch_shapes=[
            buf(3, slots, rows, width),
            buf(2, 2, n_fs, hd, rows), buf(4, 2, n_fs, hd, rows), buf(n_fs, hd, 4 * rows),
            buf(4 * rows, half), buf(n_fs, hd, half), buf(2, nz, hd, half),
            buf(2, nz // 2, hd, half), buf(2, nz // 2, hd, half), buf(nz, hd, half),
            buf(4, rows, half), buf(4, rows, half), pltpu.VMEM((rows, half), F32),
            buf(shard, width), pltpu.VMEM((4 * n_fs, 1, LANES), F32), buf(n_fs, hd, rows),
            one, sem(nz), one, one, sem(2), one, one, sem(chunks), sem(chunks), sem(chunks), sem(chunks), sem(chunks), one,
            sem(4, nz // 2), sem(2),
            one, one, one, sem(3), one, one, sem(4), pltpu.SemaphoreType.REGULAR((nz - 2,)),
        ],
        compiler_params=pltpu.CompilerParams(collective_id=0, has_side_effects=True),
    )(block_len, target, queries, keys, values, cotangent, out_weight)
    return pl.pallas_call(
        settle,
        out_shape=(
            jax.ShapeDtypeStruct(cotangent.shape, BF16),
            jax.ShapeDtypeStruct((shard, width), F32),
        ),
        in_specs=[vmem] * 3,
        out_specs=(vmem, vmem),
    )(embedding, rows_sum, factor)


def solution(mesh):
    n_dp, n_fs = mesh.shape["dp"], mesh.shape["fsdp"]
    group = math.gcd(n_dp, 4)
    quad = n_dp == 4 and n_fs % 4 == 0 and HEADS == 2 * n_fs
    both = P(("dp", "fsdp"), None, None)
    flat = P(("dp", "fsdp"))
    return jax.shard_map(
        functools.partial(local_quad, n_fs) if quad else functools.partial(local, n_dp, n_fs, group),
        mesh=mesh,
        in_specs=(both, both, both, flat, flat, both, P("fsdp", None)),
        out_specs=(both, P("fsdp", None)),
        check_vma=False,
    )
```

```python
import functools
import math

import jax
import jax.numpy as jnp
from jax import lax
from jax.experimental import pallas as pl
from jax.experimental.pallas import tpu as pltpu
from jax.sharding import PartitionSpec as P

HEADS = 16
LANES = 128
MESH = pl.DeviceIdType.MESH
F32 = jnp.float32
BF16 = jnp.bfloat16


def starts_of(width, group):
    tiles = width // LANES
    window = -(-tiles // group) * LANES
    return window, [min(i * window, width - window) for i in range(group)]


def marks_of(width):
    tiles = width // LANES
    return [tiles * tenths // 10 * LANES for tenths in (0, 4, 7, 9, 10)]


def kernel(
    n_dp, n_fs, group, finish,
    len_ref, tgt_ref, q_ref, k_ref, v_ref, cot_ref, w_ref,
    emb_ref, grad_ref, factor_ref,
    wq, cq, mine, nxt, arr, placed, gpart, yrecv, zsend, zrecv, esend, ebuf, tbuf, sbuf, srecv, gsum,
    wz_s, wz_r, wy_s, wy_r, c_s, c_r, n_s, n_r, p_s, p_r, gy_s, gy_r, gz_s, gz_r,
    e_s, e_r, t_s, t_r, q_s, q_r, m_s, m_r,
):
    slots, rows, width = q_ref.shape
    shard = w_ref.shape[0]
    hd = width // HEADS
    window, starts = starts_of(width, group)
    over = group * window - width
    nz = n_fs // 2
    d, f = lax.axis_index("dp"), lax.axis_index("fsdp")
    base = (d // group) * group
    gi = d - base
    z, y = f // 2, f % 2
    other = z * 2 + (1 - y)
    ahead, behind = (d + 1) % n_dp, (d + n_dp - 1) % n_dp
    mates = [(gi + j) % group for j in range(1, group)]
    core, side = gi % 2, gi // 2
    partner, across = side * 2 + (1 - core), (1 - side) * 2 + core

    def start_of(i):
        if group == 1:
            return 0
        return pl.multiple_of(i * window - (i // (group - 1)) * over, LANES)

    def copy(src, dst, s, r, to):
        return pltpu.make_async_remote_copy(
            src_ref=src, dst_ref=dst, send_sem=s, recv_sem=r, device_id=to, device_id_type=MESH
        )

    def spread(at, s, r):
        to = [partner, across] if group == 4 else mates
        made = [copy(at(gi), at(gi), s(j), r(j), (base + m, f)) for j, m in enumerate(to)]
        for c in made:
            c.start()
        return made

    def relay(made, at, s, r):
        if group != 4:
            return made
        made[1].wait_recv()
        c = copy(at(across), at(across), s(2), r(2), (base + partner, f))
        c.start()
        made.append(c)
        return [made[0], c]

    barrier = pltpu.get_barrier_semaphore()
    peers = [(ahead, f), (behind, f)]
    peers += [(base + m, f) for m in mates]
    peers += [(d, (f + j) % n_fs) for j in range(1, n_fs)]
    for peer in peers:
        pl.semaphore_signal(barrier, inc=1, device_id=peer, device_id_type=MESH)

    my_cols = pl.ds(start_of(gi), window)
    my_rows = pl.ds(pl.multiple_of(gi * rows, rows), rows)

    def w_at(index):
        return wq.at[pl.ds(pl.multiple_of(index * shard, shard), shard), :]

    wz, wy, cots = [], [], []

    def open_links():
        pl.semaphore_wait(barrier, len(peers))
        w_src = w_ref.at[:, my_cols]
        for j in range(1, nz):
            c = copy(w_src, w_at(f), wz_s.at[j], wz_r.at[j], (d, ((z + j) % nz) * 2 + y))
            c.start()
            wz.append(c)
        wy.append(copy(w_src, w_at(f), wy_s.at[0], wy_r.at[0], (d, other)))
        wy[0].start()
        for j, m in enumerate(mates):
            c = copy(
                cot_ref.at[0, :, pl.ds(start_of(m), window)], cq.at[my_rows, :],
                c_s.at[j], c_r.at[j], (base + m, f),
            )
            c.start()
            cots.append(c)
        wq[pl.ds(pl.multiple_of(f * shard, shard), shard), :] = w_ref[:, my_cols]
        cq[my_rows, :] = cot_ref[0, :, my_cols]

    key_pos = lax.broadcasted_iota(jnp.int32, (rows, rows), 1)
    row_pos = lax.broadcasted_iota(jnp.int32, (rows, LANES), 0)
    lens = [len_ref[s] for s in range(slots)]
    usable = [key_pos < lens[s] for s in range(slots)]
    limit = [[jnp.where(tgt_ref[s] == t, lens[s], 0) for s in range(slots)] for t in range(2)]
    keep = [[row_pos < limit[t][s] for s in range(slots)] for t in range(2)]
    tiles = {}
    marks = marks_of(width)
    parts = len(marks) - 1
    nexts, cast_all = [], []

    def send_next(part):
        cols = pl.ds(marks[part], marks[part + 1] - marks[part])
        c = copy(nxt.at[:, cols], arr.at[:, cols], n_s.at[part], n_r.at[part], (ahead, f))
        c.start()
        nexts.append(c)

    def placed_at(part):
        cols = pl.ds(marks[part], marks[part + 1] - marks[part])
        return lambda i: placed.at[pl.ds(pl.multiple_of(i * rows, rows), rows), cols]

    def cast(part):
        nexts[part].wait_recv()
        cols = pl.ds(marks[part], marks[part + 1] - marks[part])
        placed[my_rows, cols] = mine[:, cols] + arr[:, cols]
        return spread(placed_at(part), lambda j: p_s.at[part, j], lambda j: p_r.at[part, j])

    def hand_on(part, made):
        return relay(
            made, placed_at(part), lambda j: p_s.at[part, j], lambda j: p_r.at[part, j]
        )

    for h in range(HEADS):
        first, last = h * hd, (h + 1) * hd
        lo, hi = first // LANES * LANES, -(-last // LANES) * LANES
        lane = lax.broadcasted_iota(jnp.int32, (rows, hi - lo), 1) + lo
        inside = (lane >= first) & (lane < last)
        for s in range(slots):
            query = jnp.where(inside, q_ref[s, :, lo:hi].astype(F32), 0.0).astype(BF16)
            scores = lax.dot_general(
                query, k_ref[s, :, lo:hi], (((1,), (1,)), ((), ())), preferred_element_type=F32
            ) * hd ** (-0.5)
            scores = jnp.where(usable[s], scores, -1e30)
            exponent = jnp.exp(scores - jnp.max(scores, axis=-1, keepdims=True))
            weights = (exponent / jnp.sum(exponent, axis=-1, keepdims=True)).astype(BF16)
            mixed = jnp.dot(weights, v_ref[s, :, lo:hi], preferred_element_type=F32)
            mixed = jnp.where(inside, mixed, 0.0)
            for t in range(lo // LANES, hi // LANES):
                piece = mixed[:, t * LANES - lo:(t + 1) * LANES - lo]
                tiles[s, t] = tiles[s, t] + piece if (s, t) in tiles else piece
        for t in range(lo // LANES, hi // LANES):
            if (t + 1) * LANES <= last:
                cols = slice(t * LANES, (t + 1) * LANES)
                for dest, ref in ((0, mine), (1, nxt)):
                    total = sum(
                        jnp.where(keep[dest][s], tiles[s, t], 0.0) for s in range(slots)
                    )
                    ref[:, cols] = total.astype(BF16)
        if h == HEADS // 8 - 1:
            open_links()
        ready = last // LANES * LANES
        while len(nexts) < parts - 1 and marks[len(nexts) + 1] <= ready:
            send_next(len(nexts))
            if len(nexts) > 1:
                cast_all.append(cast(len(nexts) - 2))
    send_next(parts - 1)
    cast_all.append(cast(parts - 2))
    waits = hand_on(0, cast_all[0])
    cast_all.append(cast(parts - 1))
    for j in range(1, nz):
        wz[j - 1].wait_recv()
        from_f = ((z + nz - j) % nz) * 2 + y
        c = copy(w_at(from_f), w_at(from_f), wy_s.at[j], wy_r.at[j], (d, other))
        c.start()
        wy.append(c)

    for part in range(1, parts):
        waits += hand_on(part, cast_all[part])
    casts = sum(cast_all, [])
    for c in cots + waits:
        c.wait_recv()

    step = 2 * LANES
    for i in range(width // step):
        gpart[i * step:(i + 1) * step, :] = lax.dot_general(
            placed[:, i * step:(i + 1) * step], cq[...], (((0,), (0,)), ((), ())),
            preferred_element_type=F32,
        ).astype(BF16)

    def g_rows(index):
        return pl.ds(pl.multiple_of(index * shard, shard), shard)

    order = list(range(1, nz)) + [0]
    gy = []
    for j in order:
        zj = (z + j) % nz
        c = copy(
            gpart.at[g_rows(zj * 2 + (1 - y)), :], yrecv.at[zj],
            gy_s.at[j], gy_r.at[j], (d, other),
        )
        c.start()
        gy.append(c)
    gz = []
    for j, c in zip(order, gy):
        zj = (z + j) % nz
        c.wait_recv()
        pair = gpart[g_rows(zj * 2 + y), :].astype(F32) + yrecv[zj].astype(F32)
        if j == 0:
            own = pair
        else:
            zsend[j] = pair.astype(BF16)
            c = copy(zsend.at[j], zrecv.at[j], gz_s.at[j], gz_r.at[j], (d, zj * 2 + y))
            c.start()
            gz.append(c)

    for c in wy:
        c.wait_recv()
    embs = []
    for i in range(group):
        esend[i] = jnp.dot(
            placed[i * rows:(i + 1) * rows, :], wq[...], preferred_element_type=F32
        ).astype(BF16)
    for j, m in enumerate(mates):
        c = copy(esend.at[m], ebuf.at[gi], e_s.at[j], e_r.at[j], (base + m, f))
        c.start()
        embs.append(c)
    ebuf[gi] = esend[gi]

    for c in gz:
        c.wait_recv()
    for j in range(1, nz):
        own = own + zrecv[j].astype(F32)
    ends = starts[1:] + [width]
    tbuf[gi] = own.astype(BF16)
    turn_at = lambda i: tbuf.at[i]
    turn_s, turn_r = (lambda j: t_s.at[j]), (lambda j: t_r.at[j])
    turns = spread(turn_at, turn_s, turn_r)
    squares = []
    if finish:
        valid = window
        for i in range(group):
            valid = jnp.where(gi == i, ends[i] - starts[i], valid)
        lane = lax.broadcasted_iota(jnp.int32, (8, LANES), 1)
        total = jnp.zeros((8, LANES), F32)
        for col in range(0, window, LANES):
            tile = own[:, col:col + LANES].astype(BF16).astype(F32)
            part = jnp.sum((tile * tile).reshape(shard // 8, 8, LANES), axis=0)
            total = total + jnp.where(lane + col < valid, part, 0.0)
        sbuf[...] = total
        for j in range(1, n_fs):
            c = copy(sbuf, srecv.at[j], q_s.at[j], q_r.at[j], (d, (f + j) % n_fs))
            c.start()
            squares.append(c)
    waits = relay(turns, turn_at, turn_s, turn_r)
    if finish:
        for j, c in zip(range(1, n_fs), squares):
            c.wait_recv()
            total = total + srecv[j]
        gsum[gi] = total
        for j, m in enumerate(mates):
            c = copy(gsum.at[gi], gsum.at[gi], m_s.at[j], m_r.at[j], (base + m, f))
            c.start()
            squares.append(c)
    for c in embs:
        c.wait_recv()
    for i in range(group):
        emb_ref[0, :, starts[i]:ends[i]] = ebuf[i, :, 0:ends[i] - starts[i]]
    for c in waits:
        c.wait_recv()
    if finish:
        for c in squares[n_fs - 1:]:
            c.wait_recv()
        total = gsum[0]
        for i in range(1, group):
            total = total + gsum[i]
        norm = jnp.sqrt(jnp.sum(total, keepdims=True) + 1e-06)
        factor = jnp.minimum(1.0, float(width) / norm)
    for i in range(group):
        grad_ref[:, starts[i]:ends[i]] = tbuf[i, :, 0:ends[i] - starts[i]]
    factor_ref[...] = jnp.broadcast_to(factor, factor_ref.shape) if finish else jnp.ones_like(factor_ref)
    for c in wz + wy + cots + nexts + casts + gy + gz + embs + turns + squares:
        c.wait_send()


CUTS = (0, 4, 8)
SPLIT = 256
DURING = {
    (0, 0): ("near", "cots0"), (0, 5): ("hop1",), (0, 7): ("send0",), (1, 3): ("join0", "cots1"),
}
AFTER = (
    "weight0", "hop2", "pass0", "more0", "comb0", "send1", "grad0", "weight1", "join1",
    "grad1", "weight2", "pass1", "more1", "red00", "red01", "comb1", "grad2", "grad3",
    "red10", "red11", "emb", "red21", "red31", "done0", "done1", "turn0", "turn1",
)


def kernel_quad(
    n_fs,
    len_ref, tgt_ref, q_ref, k_ref, v_ref, cot_ref, w_ref,
    emb_ref, grad_ref, factor_ref,
    qkv, att, got, placed, cots, wq, gpart, yrecv, zsend, zrecv, esend, ebuf, eown, turned, srecv,
    joined, w_s, wz_r, wy_r, c_s, c_r, k_s, f_s, kx_r, ks_r, kc_r, kf_r, j_r, g_s, gy_r, gz_r, e_s, e_r, t_s, t_r, q_s, q_r,
    l_s, hop,
):
    slots, rows, width = q_ref.shape
    hd = width // HEADS
    half = width // 2
    nz = n_fs // 2
    nh = nz // 2
    per = n_fs // 2
    d, f = lax.axis_index("dp"), lax.axis_index("fsdp")
    x, c = d // 2, d % 2
    z, y = f // 2, f % 2
    partner, across = 2 * x + 1 - c, 2 * (1 - x) + c
    other = 2 * z + 1 - y
    halves = [1 - z // nh, z // nh]

    def copy(src, dst, s, r, to):
        return pltpu.make_async_remote_copy(
            src_ref=src, dst_ref=dst, send_sem=s, recv_sem=r, device_id=to, device_id_type=MESH
        )

    def start(*args):
        made = copy(*args)
        made.start()
        return made

    def landed(dst, r):
        copy(dst, dst, w_s, r, (d, f)).wait_recv()

    def left(src, s):
        copy(src, src, s, wy_r, (d, f)).wait_send()

    barrier = pltpu.get_barrier_semaphore()
    up, down = z + 1 < nz, z > 0
    beside = up.astype(jnp.int32) + down.astype(jnp.int32)

    def both_sides(sem):
        @pl.when(up)
        def _():
            pl.semaphore_signal(sem, inc=1, device_id=(d, f + 2), device_id_type=MESH)

        @pl.when(down)
        def _():
            pl.semaphore_signal(sem, inc=1, device_id=(d, f - 2), device_id_type=MESH)

    peers = [((d + i) % 4, f) for i in range(1, 4)] + [(d, other)]
    for peer in peers:
        pl.semaphore_signal(barrier, inc=1, device_id=peer, device_id_type=MESH)
    both_sides(barrier)

    def side(i):
        return pl.ds(pl.multiple_of(i * half, LANES), half)

    def shard_half(i):
        return pl.ds(pl.multiple_of(i * hd, 16), hd)

    def block(i):
        return pl.ds(pl.multiple_of(i * rows, rows), rows)

    for t in range(2):
        for n, ref in enumerate((q_ref, k_ref, v_ref)):
            at = side(halves[t])
            pltpu.make_async_copy(ref.at[:, :, at], qkv.at[n, :, :, at], l_s.at[t]).start()
    w_src = w_ref.at[shard_half(x), side(c)]
    own_w = pltpu.make_async_copy(w_src, wq.at[f], l_s.at[2])
    own_cot = pltpu.make_async_copy(cot_ref.at[0, :, side(c)], cots.at[block(d), :], l_s.at[3])
    own_w.start()
    own_cot.start()

    pieces = ((0, SPLIT), (SPLIT, half))
    low = z // nh

    def z_place(n):
        if n < nh - 1:
            return low * nh + (z % nh + 1 + n) % nh
        n = n - (nh - 1)
        return low * (nh - 1 - n) + (1 - low) * (nh + n)

    def send_beside(way, there):
        @pl.when(there)
        def _():
            start(w_src, wq.at[f], w_s, wz_r.at[z], (d, (z + way) * 2 + y))

    def open_near():
        pl.semaphore_wait(barrier, len(peers) + beside)
        both_sides(hop.at[0])
        start(w_src, wq.at[f], w_s, wy_r, (d, other))
        send_beside(1, up)
        send_beside(-1, down)

    def open_far(n):
        pl.semaphore_wait(hop.at[n - 1], beside)
        if n < nz - 2:
            both_sides(hop.at[n])
        send_beside(n + 1, z + n + 1 < nz)
        send_beside(-n - 1, z > n)

    def send_cots(p):
        a, b = pieces[p]
        for j in (2, 1, 3):
            m = (d + j) % 4
            at = pl.ds(pl.multiple_of((m % 2) * half + a, LANES), b - a)
            start(cot_ref.at[0, :, at], cots.at[block(d), a:b], c_s, c_r.at[p], (m, f))

    def pass_weight(n):
        from_z = z_place(n)
        here = wq.at[from_z * 2 + y]
        landed(here, wz_r.at[from_z])
        start(here, here, w_s, wy_r, (d, other))

    key_pos = lax.broadcasted_iota(jnp.int32, (rows, rows), 0)
    row_pos = lax.broadcasted_iota(jnp.int32, (hd, rows), 1)
    lens = [len_ref[s] for s in range(slots)]
    usable = [key_pos < lens[s] for s in range(slots)]
    keep = [
        [row_pos < jnp.where(tgt_ref[s] == t, lens[s], 0) for s in range(slots)] for t in range(2)
    ]
    scale = hd ** (-0.5) * math.log2(math.e)
    turned_v = {}

    def value_rows(step, s, first, last):
        found = []
        for t in range(first // LANES, -(-last // LANES)):
            if (step, s, t) not in turned_v:
                at = pl.ds(pl.multiple_of(halves[step] * half + t * LANES, LANES), LANES)
                turned_v[step, s, t] = qkv[2, s, :, at].T
            a, b = max(first - t * LANES, 0), min(last - t * LANES, LANES)
            found.append(turned_v[step, s, t][a:b, :])
        return found[0] if len(found) == 1 else jnp.concatenate(found, axis=0)

    def attend(step, h):
        first, last = h * hd, (h + 1) * hd
        lo, hi = first // LANES * LANES, -(-last // LANES) * LANES
        at = pl.ds(pl.multiple_of(halves[step] * half + lo, LANES), hi - lo)
        lane = lax.broadcasted_iota(jnp.int32, (rows, hi - lo), 1) + lo
        inside = ((lane >= first) & (lane < last)).astype(F32).astype(BF16)
        mixed = []
        for s in range(slots):
            scores = lax.dot_general(
                qkv[1, s, :, at], qkv[0, s, :, at] * inside, (((1,), (1,)), ((), ())),
                preferred_element_type=F32,
            )
            scores = jnp.where(usable[s], scores, -1e30)
            exponent = jnp.exp2((scores - jnp.max(scores, axis=0, keepdims=True)) * scale)
            inverse = 1.0 / jnp.sum(exponent, axis=0, keepdims=True)
            weights = (exponent * inverse).astype(BF16)
            mixed.append(jnp.dot(
                value_rows(step, s, first, last), weights, preferred_element_type=F32
            ))
        for t in range(2):
            total = sum(jnp.where(keep[t][s], mixed[s], 0.0) for s in range(slots))
            att[t, h % 2, step * per + h // 2] = total.astype(BF16)

    cuts = CUTS

    def part_of(k, i):
        n = (cuts[k + 1] - cuts[k]) // 2
        return pl.ds(cuts[k] + i * n, n)

    def send_chunk(k):
        at = pl.ds(cuts[k], cuts[k + 1] - cuts[k])
        start(att.at[c, 1 - x, at], got.at[d, c, at], k_s, kx_r.at[k], (across, f))
        theirs = part_of(k, 1 - c)
        start(att.at[1 - c, 1 - x, theirs], joined.at[theirs], f_s, j_r.at[k], (partner, f))
        start(att.at[:, x, at], got.at[d, :, at], k_s, kc_r.at[k], (partner, f))
        for t in range(2):
            got[d, t, at] = att[t, x, at]

    def join_chunk(k):
        ours = part_of(k, c)
        landed(joined.at[ours], j_r.at[k])
        joined[ours] = joined[ours] + att[1 - c, 1 - x, ours]
        start(joined.at[ours], got.at[2 * x + 1, 0, ours], f_s, ks_r.at[k], (across, f))

    def pass_chunk(k):
        here = got.at[across, c, pl.ds(cuts[k], cuts[k + 1] - cuts[k])]
        landed(here, kx_r.at[k])
        start(here, here, f_s, kf_r.at[k], (partner, f))

    def pass_joined(k):
        here = got.at[2 * (1 - x) + 1, 0, part_of(k, c)]
        landed(here, ks_r.at[k])
        start(here, here, f_s, kf_r.at[k], (partner, f))

    def combine(k):
        n = cuts[k + 1] - cuts[k]
        landed(got.at[0, :, 0:n], kc_r.at[k])
        landed(got.at[0, 0, 0:n + n // 2], kf_r.at[k])
        for s in range(cuts[k], cuts[k + 1]):
            index = halves[s // per] * per + s % per
            for b in range(4):
                placed[index, :, b * rows:(b + 1) * rows] = got[b, 0, s] + got[(b + 3) % 4, 1, s]

    gy = {}
    parts = [(step, *piece) for step in range(2) for piece in pieces]

    def gradient(p):
        step, a, b = parts[p]
        mat = placed[pl.ds(halves[step] * per, per)].reshape(per * hd, 4 * rows)
        gpart[step, :, :, a:b] = jnp.dot(
            mat, cots[:, a:b], preferred_element_type=F32
        ).astype(BF16).reshape(per, hd, b - a)
        for r in order(step):
            if step == 0 or r:
                trade(p, r)

    def trade(p, r):
        step, a, b = parts[p]
        i = place(step, r)
        gy[p, r] = start(
            gpart.at[step, 2 * i + 1 - y, :, a:b], yrecv.at[step, i, :, a:b],
            g_s, gy_r.at[p, r], (d, other),
        )

    def order(step):
        return list(range(nh)) if step == 0 else list(range(1, nh)) + [0]

    def place(step, r):
        return r if step == 0 else (z % nh + r) % nh

    def reduce(p, r):
        step, a, b = parts[p]
        i = place(step, r)
        gy[p, r].wait_recv()
        pair = gpart[step, 2 * i + y, :, a:b].astype(F32) + yrecv[step, i, :, a:b].astype(F32)
        if step == 1 and r == 0:
            return pair
        to = halves[step] * nh + i
        j = (to - z + nz) % nz
        zsend[step, r, :, a:b] = pair.astype(BF16)
        start(
            zsend.at[step, r, :, a:b], zrecv.at[j, :, a:b], g_s, gz_r.at[p % 2], (d, 2 * to + y),
        )

    def gradient_in(p):
        if p < 2:
            a, b = pieces[p]
            landed(cots.at[0:3 * rows, a:b], c_r.at[p])
            if p == 0:
                own_cot.wait()
        gradient(p)
        if p == 3:
            trade(2, 0)
            trade(3, 0)

    def embed():
        own_w.wait()
        landed(wq.at[0:nz], wy_r)
        wmat = wq[...].reshape(half, half)
        for j in (2, 3, 1, 0):
            m = (d + j) % 4
            part = lax.dot_general(
                placed[:, :, block(m)].reshape(half, rows), wmat, (((0,), (0,)), ((), ())),
                preferred_element_type=F32,
            )
            if j == 0:
                eown[...] = part
            else:
                esend[j] = part.astype(BF16)
                start(esend.at[j], ebuf.at[d], e_s, e_r, (m, f))

    def turn_at(i, q):
        a, b = pieces[q]
        at = pl.ds(pl.multiple_of((i % 2) * half + a, LANES), b - a)
        return turned.at[shard_half(i // 2), at]

    me = d * n_fs + f
    squares = []

    def finish(q):
        a, b = pieces[q]
        own = reduce(2 + q, 0)
        landed(zrecv.at[0:nz - 1, :, a:b], gz_r.at[q])
        for j in range(1, nz):
            own = own + zrecv[j, :, a:b].astype(F32)
        turn_at(d, q)[...] = own.astype(BF16)
        start(turn_at(d, q), turn_at(d, q), t_s, t_r.at[q], (across, f))
        start(turn_at(d, q), turn_at(d, q), t_s, t_r.at[2], (partner, f))
        square = jnp.sum(own * own, axis=0, keepdims=True)
        squares.extend(square[:, i:i + LANES] for i in range(0, b - a, LANES))
        if b == half:
            srecv[me] = sum(squares)
            for n in reversed(range(-1, nz - 1)):
                to = z_place(n) if n >= 0 else z
                for k in range(1 if n < 0 else 0, 8):
                    peer = ((d + k // 2) % 4, 2 * to + (y + k) % 2)
                    start(srecv.at[me], srecv.at[me], q_s, q_r, peer)

    def pass_turn(q):
        landed(turn_at(across, q), t_r.at[q])
        start(turn_at(across, q), turn_at(across, q), t_s, t_r.at[2], (partner, f))

    acts = {"near": open_near, "emb": embed}
    for p in range(4):
        acts[f"grad{p}"] = functools.partial(gradient_in, p)
        for r in range(nh):
            acts[f"red{p}{r}"] = functools.partial(reduce, p, r)
    for p in range(2):
        acts[f"cots{p}"] = functools.partial(send_cots, p)
        acts[f"done{p}"] = functools.partial(finish, p)
        acts[f"turn{p}"] = functools.partial(pass_turn, p)
    for n in range(nz - 1):
        acts[f"weight{n}"] = functools.partial(pass_weight, n)
        acts[f"hop{n + 1}"] = functools.partial(open_far, n + 1)
    for k in range(len(cuts) - 1):
        acts[f"send{k}"] = functools.partial(send_chunk, k)
        acts[f"join{k}"] = functools.partial(join_chunk, k)
        acts[f"pass{k}"] = functools.partial(pass_chunk, k)
        acts[f"more{k}"] = functools.partial(pass_joined, k)
        acts[f"comb{k}"] = functools.partial(combine, k)

    got[2 * (1 - x), 1] = jnp.zeros_like(got[0, 0])
    for step in range(2):
        here = qkv.at[:, :, :, 0:half]
        pltpu.make_async_copy(here, here, l_s.at[step]).wait()
        for h in range(2 * per):
            attend(step, h)
            for name in DURING.get((step, h), ()):
                acts[name]()
    for name in AFTER:
        acts[name]()

    landed(esend.at[0:3], e_r)
    emb_ref[0, :, side(c)] = (eown[...] + ebuf[across].astype(F32)).astype(BF16)
    emb_ref[0, :, side(1 - c)] = (
        ebuf[partner].astype(F32) + ebuf[2 * (1 - x) + 1 - c].astype(F32)
    ).astype(BF16)
    landed(wq.at[0:2], t_r.at[2])
    grad_ref[...] = turned[...]
    landed(srecv.at[0:4 * n_fs - 1], q_r)
    norm = jnp.sqrt(jnp.sum(jnp.sum(srecv[...], axis=0), keepdims=True) + 1e-06)
    factor_ref[...] = jnp.broadcast_to(jnp.minimum(1.0, float(width) / norm), factor_ref.shape)
    left(wq.at[0:2 * nz - 1], w_s)
    left(cots.at[0:3 * rows], c_s)
    left(got.at[0:3, 0], k_s)
    left(got.at[0:2, :, 0:n_fs * 5 // 8], f_s)
    left(wq.at[0:2 * nz - 1], g_s)
    left(esend.at[0:3], e_s)
    left(wq.at[0:3], t_s)
    left(srecv.at[0:4 * n_fs - 1], q_s)


def settle(emb_ref, rows_ref, factor_ref, emb_out, grad_out):
    emb_out[...] = emb_ref[...]
    grad_out[...] = rows_ref[...].astype(F32) * factor_ref[0:1, 0:1]


def local(n_dp, n_fs, group, queries, keys, values, block_len, target, cotangent, out_weight):
    slots, rows, width = queries.shape
    shard = out_weight.shape[0]
    window, starts = starts_of(width, group)
    nz = n_fs // 2
    finish = group == n_dp
    vmem = pl.BlockSpec(memory_space=pltpu.VMEM)
    smem = pl.BlockSpec(memory_space=pltpu.SMEM)
    sem = lambda *shape: pltpu.SemaphoreType.DMA(shape)
    mates = max(group - 1, 1)
    parts = len(marks_of(width)) - 1
    embedding, rows_sum, factor = pl.pallas_call(
        functools.partial(kernel, n_dp, n_fs, group, finish),
        out_shape=(
            jax.ShapeDtypeStruct(cotangent.shape, BF16),
            jax.ShapeDtypeStruct((shard, width), BF16),
            jax.ShapeDtypeStruct((8, LANES), F32),
        ),
        in_specs=[smem, smem] + [vmem] * 5,
        out_specs=(vmem, vmem, vmem),
        scratch_shapes=[
            pltpu.VMEM((width, window), BF16),
            pltpu.VMEM((group * rows, window), BF16),
            pltpu.VMEM((rows, width), BF16),
            pltpu.VMEM((rows, width), BF16),
            pltpu.VMEM((rows, width), BF16),
            pltpu.VMEM((group * rows, width), BF16),
            pltpu.VMEM((width, window), BF16),
            pltpu.VMEM((nz, shard, window), BF16),
            pltpu.VMEM((nz, shard, window), BF16),
            pltpu.VMEM((nz, shard, window), BF16),
            pltpu.VMEM((group, rows, window), BF16),
            pltpu.VMEM((group, rows, window), BF16),
            pltpu.VMEM((group, shard, window), BF16),
            pltpu.VMEM((8, LANES), F32),
            pltpu.VMEM((n_fs, 8, LANES), F32),
            pltpu.VMEM((group, 8, LANES), F32),
            sem(nz), sem(nz), sem(nz), sem(nz), sem(mates), sem(mates), sem(parts), sem(parts),
            sem(parts, mates), sem(parts, mates), sem(nz), sem(nz), sem(nz), sem(nz),
            sem(mates), sem(mates), sem(mates), sem(mates), sem(n_fs), sem(n_fs),
            sem(mates), sem(mates),
        ],
        compiler_params=pltpu.CompilerParams(collective_id=0, has_side_effects=True),
    )(block_len, target, queries, keys, values, cotangent, out_weight)
    embedding, grad = pl.pallas_call(
        settle,
        out_shape=(
            jax.ShapeDtypeStruct(cotangent.shape, BF16),
            jax.ShapeDtypeStruct((shard, width), F32),
        ),
        in_specs=[vmem] * 3,
        out_specs=(vmem, vmem),
    )(embedding, rows_sum, factor)
    if not finish:
        lines = [[i for i in range(n_dp) if i % group == g] for g in range(group)]
        grad = lax.psum(grad, "dp", axis_index_groups=lines)
        squares = lax.psum(jnp.sum(grad * grad), "fsdp")
        grad = grad * jnp.minimum(1.0, float(width) / jnp.sqrt(squares + 1e-06))
    return embedding, grad


def local_quad(n_fs, queries, keys, values, block_len, target, cotangent, out_weight):
    slots, rows, width = queries.shape
    shard = out_weight.shape[0]
    hd, half, nz = width // HEADS, width // 2, n_fs // 2
    vmem = pl.BlockSpec(memory_space=pltpu.VMEM)
    smem = pl.BlockSpec(memory_space=pltpu.SMEM)
    sem = lambda *shape: pltpu.SemaphoreType.DMA(shape)
    one = pltpu.SemaphoreType.DMA
    buf = lambda *shape: pltpu.VMEM(shape, BF16)
    chunks = len(CUTS) - 1
    embedding, rows_sum, factor = pl.pallas_call(
        functools.partial(kernel_quad, n_fs),
        out_shape=(
            jax.ShapeDtypeStruct(cotangent.shape, BF16),
            jax.ShapeDtypeStruct((shard, width), BF16),
            jax.ShapeDtypeStruct((8, LANES), F32),
        ),
        in_specs=[smem, smem] + [pl.BlockSpec(memory_space=pltpu.HBM)] * 5,
        out_specs=(vmem, vmem, vmem),
        scratch_shapes=[
            buf(3, slots, rows, width),
            buf(2, 2, n_fs, hd, rows), buf(4, 2, n_fs, hd, rows), buf(n_fs, hd, 4 * rows),
            buf(4 * rows, half), buf(n_fs, hd, half), buf(2, nz, hd, half),
            buf(2, nz // 2, hd, half), buf(2, nz // 2, hd, half), buf(nz, hd, half),
            buf(4, rows, half), buf(4, rows, half), pltpu.VMEM((rows, half), F32),
            buf(shard, width), pltpu.VMEM((4 * n_fs, 1, LANES), F32), buf(n_fs, hd, rows),
            one, sem(nz), one, one, sem(2), one, one, sem(chunks), sem(chunks), sem(chunks), sem(chunks), sem(chunks), one,
            sem(4, nz // 2), sem(2),
            one, one, one, sem(3), one, one, sem(4), pltpu.SemaphoreType.REGULAR((nz - 2,)),
        ],
        compiler_params=pltpu.CompilerParams(collective_id=0, has_side_effects=True),
    )(block_len, target, queries, keys, values, cotangent, out_weight)
    return pl.pallas_call(
        settle,
        out_shape=(
            jax.ShapeDtypeStruct(cotangent.shape, BF16),
            jax.ShapeDtypeStruct((shard, width), F32),
        ),
        in_specs=[vmem] * 3,
        out_specs=(vmem, vmem),
    )(embedding, rows_sum, factor)


def solution(mesh):
    n_dp, n_fs = mesh.shape["dp"], mesh.shape["fsdp"]
    group = math.gcd(n_dp, 4)
    quad = n_dp == 4 and n_fs % 4 == 0 and HEADS == 2 * n_fs
    both = P(("dp", "fsdp"), None, None)
    flat = P(("dp", "fsdp"))
    return jax.shard_map(
        functools.partial(local_quad, n_fs) if quad else functools.partial(local, n_dp, n_fs, group),
        mesh=mesh,
        in_specs=(both, both, both, flat, flat, both, P("fsdp", None)),
        out_specs=(both, P("fsdp", None)),
        check_vma=False,
    )
```
